768 devices in a mesh: dap: 96 (over x, z, y_lo), section: 8 (over y_hi, core).
Axes of the slice: x: 4, y: 8 (y_hi: 4, y_lo: 2; y = y_hi * 2 + y_lo), z: 12, core: 2. Of those that a mesh axis runs over, the one named last changes fastest.
Arguments:
- alignment_state_new: float32 [8, 384, 384, 256], P('section', 'dap'), may hold values from -8 to 8
- residue_grid_new: float32 [8, 384, 384, 128], P('section', 'dap'), may hold values from -8 to 8
- stacked_projection_weights: bfloat16 [8, 256, 1024], P('section'), may hold values from -0.375 to 0.375
- outgoing_weight_matrix: bfloat16 [8, 256, 256], P('section'), may hold values from -0.375 to 0.375
- grid_logit_matrix: bfloat16 [8, 128, 8], P('section'), may hold values from -14 to 14, as said below
- layernorm_gain_vector: float32 [8, 256], P('section'), may hold values from 0.5 to 1.5
- grid_scale_factor: float32 [8, 128], P('section'), may hold values from 0.5 to 1.5
- sigmoid_offset: float32 [8, 256], P('section'), may hold values from -1 to 2
- outgoing_bias_vector: float32 [8, 256], P('section'), may hold values from -3 to 3
Outputs:
- alignment_after_attention: float32 [8, 384, 384, 256], P('section', 'dap')
- grid_state_handed: float32 [8, 384, 384, 128], P('section', 'dap')
The draws below stay inside these ranges and needn't reach their ends.
Inputs may be any that keep to these rules, and one draw needn't show every extreme that they name: `grid_logit_matrix`: pair-bias projection weights.
All inputs are finite; a program needn't handle non-finite values.
Results may differ from the reference program's by a relative error of at most 0.0053.
Values may be sent and summed in bfloat16 or wider, within the bound.
A program may use at most 128 MiB of HBM per device.

```python
import math
import jax
import jax.numpy as jnp
from jax import lax

CHANNEL_WIDTH = 256
C_Z = 128
HEAD_NUMBER = 8
SINGLE_HEAD_SIZE = 32
WINDOW_LENGTH = 384
HOMOLOG_COUNT = 384
PORTION_TOTAL = 8


def shared_pattern(key):
    folded = jax.random.fold_in(key, 9173)
    stochastic_seed_parts = jax.random.split(folded, 7)
    positions = jnp.arange(WINDOW_LENGTH, dtype=jnp.float32) / WINDOW_LENGTH
    frequencies = jax.random.uniform(stochastic_seed_parts[0], (PORTION_TOTAL, 4, 1), jnp.float32, 0.5, 3.0)
    phases = jax.random.uniform(stochastic_seed_parts[1], (PORTION_TOTAL, 4, 1), jnp.float32, -math.pi, math.pi)
    residue_profile = jnp.sum(jnp.cos(2.0 * math.pi * frequencies * positions[None, None, :] + phases), axis=1) / math.sqrt(2.0)
    pairwise_direction = jnp.clip(jax.random.normal(stochastic_seed_parts[2], (PORTION_TOTAL, C_Z), jnp.float32), -3.0, 3.0)
    homolog_orient = jnp.clip(jax.random.normal(stochastic_seed_parts[3], (PORTION_TOTAL, CHANNEL_WIDTH), jnp.float32), -3.0, 3.0)
    distance_direction = jnp.clip(jax.random.normal(stochastic_seed_parts[4], (PORTION_TOTAL, C_Z), jnp.float32), -3.0, 3.0)
    distance_wave = jax.random.uniform(stochastic_seed_parts[5], (PORTION_TOTAL, 1, 1), jnp.float32, 1.0, 4.0)
    distance_phase = jax.random.uniform(stochastic_seed_parts[6], (PORTION_TOTAL, 1, 1), jnp.float32, -math.pi, math.pi)
    return (residue_profile, pairwise_direction, homolog_orient, distance_direction, distance_wave, distance_phase)


def draw_residue_grid_new(key, part):
    residue_profile, pairwise_direction, homolog_orient, distance_direction, distance_wave, distance_phase = shared_pattern(key)
    jitter_key = jax.random.fold_in(key, 4111)
    grid_shape = (PORTION_TOTAL, WINDOW_LENGTH, WINDOW_LENGTH, C_Z)
    random_jitter = jnp.clip(jax.random.normal(jitter_key, grid_shape, jnp.float32), -4.0, 4.0)
    residues = jnp.arange(WINDOW_LENGTH, dtype=jnp.float32)
    offsets = (residues[:, None] - residues[None, :]) / WINDOW_LENGTH
    spacing = jnp.cos(2.0 * math.pi * distance_wave * offsets[None, :, :] + distance_phase)
    grid = random_jitter + residue_profile[:, None, :, None] * pairwise_direction[:, None, None, :]
    grid = grid + 0.8 * spacing[:, :, :, None] * distance_direction[:, None, None, :]
    return jnp.clip(grid, -8.0, 8.0)


def draw_alignment_state_new(key, part):
    residue_profile, pairwise_direction, homolog_orient, distance_direction, distance_wave, distance_phase = shared_pattern(key)
    jitter_key = jax.random.fold_in(key, 4219)
    factor_key = jax.random.fold_in(key, 4327)
    homolog_extent = (PORTION_TOTAL, HOMOLOG_COUNT, WINDOW_LENGTH, CHANNEL_WIDTH)
    random_jitter = jnp.clip(jax.random.normal(jitter_key, homolog_extent, jnp.float32), -4.0, 4.0)
    row_multiplier = jax.random.uniform(factor_key, (PORTION_TOTAL, HOMOLOG_COUNT, 1, 1), jnp.float32, 0.6, 1.4)
    alignment_input = random_jitter + 1.5 * row_multiplier * residue_profile[:, None, :, None] * homolog_orient[:, None, None, :]
    return jnp.clip(alignment_input, -8.0, 8.0)


def draw_grid_logit_matrix(key, part):
    residue_profile, pairwise_direction, homolog_orient, distance_direction, distance_wave, distance_phase = shared_pattern(key)
    jitter_key = jax.random.fold_in(key, 5501)
    sign_key = jax.random.fold_in(key, 5407)
    scale_key = jax.random.fold_in(key, 5303)
    random_jitter = jnp.clip(jax.random.normal(jitter_key, (PORTION_TOTAL, C_Z, HEAD_NUMBER), jnp.float32), -4.0, 4.0)
    head_sign = 2.0 * jax.random.bernoulli(sign_key, 0.5, (PORTION_TOTAL, 1, HEAD_NUMBER)).astype(jnp.float32) - 1.0
    head_scale = jnp.exp(jax.random.uniform(scale_key, (PORTION_TOTAL, 1, HEAD_NUMBER), jnp.float32, jnp.log(0.5), jnp.log(3.0)))
    mixed = 0.8 * random_jitter + 1.5 * head_sign * pairwise_direction[:, :, None] / C_Z ** 0.5
    scaled = jnp.clip(mixed * head_scale / C_Z ** 0.5, -14.0, 14.0)
    return scaled.astype(jnp.bfloat16)


def steps_of(own_key, dims, cuts, smallest, top_value):
    def one(axis_at, blocks):
        draws = jax.random.uniform(jax.random.fold_in(jax.random.fold_in(own_key, 6), axis_at), (blocks,), jnp.float32, smallest / len(cuts), top_value / len(cuts))
        return jnp.repeat(jnp.exp(draws), dims[axis_at] // blocks).reshape((-1,) + (1,) * (len(dims) - axis_at - 1))

    factor_of = one(*cuts[0])
    for cut in cuts[1:]:
        factor_of = factor_of * one(*cut)
    return factor_of


def noise(own_key, shape, scale, limit, pieces=(), kind=jnp.bfloat16):
    entries = scale * jax.random.normal(own_key, shape, jnp.float32)
    if pieces:
        entries = entries * steps_of(own_key, shape, pieces, -0.22, 0.18)
    return jnp.clip(entries, -limit, limit).astype(kind)


def setup_inputs(seed: int = 0) -> dict:
    streams_of = jax.random.split(jax.random.key(seed), 10)
    return {
        "alignment_state_new": draw_alignment_state_new(jax.random.fold_in(streams_of[9], 71), 0),
        "residue_grid_new": draw_residue_grid_new(jax.random.fold_in(streams_of[9], 71), 0),
        "stacked_projection_weights": noise(streams_of[2], (PORTION_TOTAL, CHANNEL_WIDTH, 4 * HEAD_NUMBER * SINGLE_HEAD_SIZE), CHANNEL_WIDTH ** -0.5, 0.375, ((0, 8),)),
        "outgoing_weight_matrix": noise(streams_of[3], (PORTION_TOTAL, HEAD_NUMBER * SINGLE_HEAD_SIZE, CHANNEL_WIDTH), (HEAD_NUMBER * SINGLE_HEAD_SIZE) ** -0.5, 0.375, ((0, 8),)),
        "grid_logit_matrix": draw_grid_logit_matrix(jax.random.fold_in(streams_of[9], 71), 0),
        "layernorm_gain_vector": jnp.clip(1.0 + 0.1 * jax.random.normal(streams_of[5], (PORTION_TOTAL, CHANNEL_WIDTH), jnp.float32), 0.5, 1.5),
        "grid_scale_factor": jnp.clip(1.0 + 0.1 * jax.random.normal(streams_of[6], (PORTION_TOTAL, C_Z), jnp.float32), 0.5, 1.5),
        "sigmoid_offset": jnp.clip(-1.0 + 3.0 * jax.random.uniform(streams_of[7], (PORTION_TOTAL, HEAD_NUMBER * SINGLE_HEAD_SIZE), jnp.float32) ** steps_of(streams_of[7], (PORTION_TOTAL, HEAD_NUMBER * SINGLE_HEAD_SIZE), ((0, 8),), -0.2, 0.2), -1.0, 2.0),
        "outgoing_bias_vector": noise(streams_of[8], (PORTION_TOTAL, CHANNEL_WIDTH), 0.5, 3.0, ((0, 8),), jnp.float32),
    }


epsilon = 1e-05

def standardize_features(values, gain):
    center = values - lax.optimization_barrier(jnp.mean(values, axis=-1, keepdims=True))
    spread = lax.optimization_barrier(jnp.mean(center * center, axis=-1, keepdims=True))
    return center * lax.rsqrt(spread + epsilon) * gain

def handoff_piece_step(joined_matrices):
    alignment_arriving, grid_state_arriving, stacked_projection_weights, outgoing_weight_matrix, grid_logit_matrix, layernorm_gain_vector, grid_scale_factor, sigmoid_offset, outgoing_bias_vector = joined_matrices
    width = HEAD_NUMBER * SINGLE_HEAD_SIZE
    pair_norm = standardize_features(grid_state_arriving, grid_scale_factor).astype(jnp.bfloat16)
    bias = jnp.einsum('ijc,ch->hij', pair_norm.astype(jnp.float32), grid_logit_matrix.astype(jnp.float32)).astype(jnp.bfloat16)
    alignment_standardized = standardize_features(alignment_arriving, layernorm_gain_vector).astype(jnp.bfloat16)
    score_scale = 1.0 / SINGLE_HEAD_SIZE ** 0.5

    def lone_line(alignment_one_line):
        mapped_lines = jnp.dot(alignment_one_line, stacked_projection_weights, preferred_element_type=jnp.float32)
        queries = mapped_lines[:, :width].astype(jnp.bfloat16).reshape(WINDOW_LENGTH, HEAD_NUMBER, SINGLE_HEAD_SIZE)
        key_rows = mapped_lines[:, width:2 * width].astype(jnp.bfloat16).reshape(WINDOW_LENGTH, HEAD_NUMBER, SINGLE_HEAD_SIZE)
        val_rows = mapped_lines[:, 2 * width:3 * width].astype(jnp.bfloat16).reshape(WINDOW_LENGTH, HEAD_NUMBER, SINGLE_HEAD_SIZE)
        gates = jax.nn.sigmoid(mapped_lines[:, 3 * width:] + sigmoid_offset)
        scores = jnp.einsum('ihd,jhd->hij', queries.astype(jnp.float32), key_rows.astype(jnp.float32)) * score_scale
        scores = scores + bias.astype(jnp.float32)
        probs = jax.nn.softmax(scores, axis=-1).astype(jnp.bfloat16)
        attended = jnp.einsum('hij,jhd->ihd', probs.astype(jnp.float32), val_rows.astype(jnp.float32)).reshape(WINDOW_LENGTH, width)
        gated = (attended * gates).astype(jnp.bfloat16)
        return jnp.dot(gated, outgoing_weight_matrix, preferred_element_type=jnp.float32) + outgoing_bias_vector
    return alignment_arriving + lax.map(lone_line, alignment_standardized)

def reference(alignment_state_new, residue_grid_new, stacked_projection_weights, outgoing_weight_matrix, grid_logit_matrix, layernorm_gain_vector, grid_scale_factor, sigmoid_offset, outgoing_bias_vector):
    alignment_arriving = jnp.roll(alignment_state_new, 1, axis=0)
    grid_state_handed = jnp.roll(residue_grid_new, 1, axis=0)
    alignment_after_attention = lax.map(handoff_piece_step, (alignment_arriving, grid_state_handed, stacked_projection_weights, outgoing_weight_matrix, grid_logit_matrix, layernorm_gain_vector, grid_scale_factor, sigmoid_offset, outgoing_bias_vector))
    return (alignment_after_attention, grid_state_handed)
```

```python
import functools

import jax
import jax.numpy as jnp
from jax import lax
from jax.experimental import pallas as pl
from jax.experimental.pallas import tpu as pltpu
from jax.sharding import PartitionSpec as P

EPSILON = 1e-05
MESH = pl.DeviceIdType.MESH
BF16 = jnp.bfloat16
F32 = jnp.float32
HALF = 128


def standardize(values, gain):
    center = values - jnp.mean(values, axis=-1, keepdims=True)
    spread = jnp.mean(center * center, axis=-1, keepdims=True)
    return center * lax.rsqrt(spread + EPSILON) * gain


def attend_row(x, bias, weights, w_out, gain, offset, out_bias, scratch, heads, dim):
    q_sc, k_sc, v_sc, gate_sc, gated_sc = scratch
    n, width = x.shape
    per_half = HALF // dim
    normed = standardize(x, gain).astype(BF16)
    member = lax.broadcasted_iota(jnp.int32, (n, HALF), 1) // dim

    def project(block):
        return jnp.dot(
            normed, weights[:, block * width : (block + 1) * width], preferred_element_type=F32
        )

    q_sc[...] = (project(0) * (1.0 / dim**0.5)).astype(BF16)
    keys = project(1)
    values = project(2)
    for h in range(heads):
        lanes = slice(h // per_half * HALF, (h // per_half + 1) * HALF)
        mine = member == h % per_half
        k_sc[h * n : (h + 1) * n, :] = jnp.where(mine, keys[:, lanes], 0.0).astype(BF16)
        v_sc[h * n : (h + 1) * n, :HALF] = jnp.where(mine, values[:, lanes], 0.0).astype(BF16)
    gate_sc[...] = jax.nn.sigmoid(project(3) + offset)
    for half in range(width // HALF):
        lanes = slice(half * HALF, (half + 1) * HALF)
        queries = q_sc[:, lanes]
        total = None
        for pair in range(per_half // 2):
            h = half * per_half + pair * 2
            scores = lax.dot_general(
                queries,
                k_sc[h * n : (h + 2) * n, :],
                (((1,), (1,)), ((), ())),
                preferred_element_type=F32,
            )
            probs = []
            for u in range(2):
                own = bias[:, :, (h + u) * n : (h + u + 1) * n].astype(F32).reshape(n, n)
                shifted = scores[:, u * n : (u + 1) * n] + own
                top = jnp.max(shifted, axis=-1, keepdims=True)
                probs.append(jnp.exp(shifted - top).astype(BF16))
            part = jnp.dot(
                jnp.concatenate(probs, axis=-1),
                v_sc[h * n : (h + 2) * n, :],
                preferred_element_type=F32,
            )
            total = part if total is None else total + part
        gated_sc[:, lanes] = (total[:, :HALF] / total[:, HALF:] * gate_sc[:, lanes]).astype(BF16)
    return x + (jnp.dot(gated_sc[...], w_out, preferred_element_type=F32) + out_bias)


def kernel(
    nx,
    nz,
    ns,
    heads,
    dim,
    msa_hbm,
    pair_hbm,
    weights_hbm,
    w_out_hbm,
    logit_ref,
    gain_ref,
    pair_gain_ref,
    offset_ref,
    out_bias_ref,
    out_hbm,
    pair_out_hbm,
    x_sc,
    pair_sc,
    w_sc,
    wo_sc,
    next_logit,
    next_gain,
    shard,
    stage,
    bias,
    q_sc,
    k_sc,
    v_sc,
    gate_sc,
    gated_sc,
    local_sem,
    w_send,
    w_recv,
    b_send,
    b_recv,
    zr_send,
    zr_recv,
    zl_send,
    zl_recv,
    xr_send,
    xr_recv,
    xl_send,
    xl_recv,
    m_send,
    m_recv,
    p_send,
    p_recv,
):
    rows, n = x_sc.shape[0], x_sc.shape[1]
    n_right = nz // 2
    n_left = nz - 1 - n_right
    d = lax.axis_index("dap")
    s = lax.axis_index("section")
    ndap = nx * nz * 2
    x = lax.div(d, 2 * nz)
    z = lax.rem(lax.div(d, 2), nz)
    low = lax.rem(d, 2)
    base = d - 2 * z
    z_right = base + 2 * lax.rem(z + 1, nz)
    z_left = base + 2 * lax.rem(z + nz - 1, nz)
    x_right = lax.rem(d + 2 * nz, ndap)
    x_left = lax.rem(d + ndap - 2 * nz, ndap)
    other = d + 1 - 2 * low
    s_next = lax.rem(s + 1, ns)
    s_prev = lax.rem(s + ns - 1, ns)

    def slot(dx, dz):
        return lax.rem(x + dx + nx, nx) * nz + lax.rem(z + dz + nz, nz)

    pair_in = pltpu.make_async_copy(pair_hbm.at[0], pair_sc, local_sem.at[0])
    w_in = pltpu.make_async_copy(weights_hbm.at[0], w_sc, local_sem.at[1])
    wo_in = pltpu.make_async_copy(w_out_hbm.at[0], wo_sc, local_sem.at[2])
    pair_in.start()
    w_in.start()
    wo_in.start()

    barrier = pltpu.get_barrier_semaphore()
    peers = (
        (z_right, s),
        (z_left, s),
        (x_right, s),
        (x_left, s),
        (d, s_next),
        (d, s_prev),
        (other, s_next),
        (other, s_prev),
    )
    for peer in peers:
        pl.semaphore_signal(barrier, inc=1, device_id=peer, device_id_type=MESH)
    pl.semaphore_wait(barrier, len(peers))

    def remote(src, dst, send, recv, peer):
        return pltpu.make_async_remote_copy(
            src_ref=src,
            dst_ref=dst,
            send_sem=send,
            recv_sem=recv,
            device_id=peer,
            device_id_type=MESH,
        )

    logit_copy = remote(logit_ref, next_logit, w_send.at[0], w_recv.at[0], (d, s_prev))
    gain_copy = remote(pair_gain_ref, next_gain, w_send.at[1], w_recv.at[1], (d, s_prev))
    logit_copy.start()
    gain_copy.start()

    def msa_copy(r):
        return remote(msa_hbm.at[0, r], x_sc.at[r], m_send.at[r], m_recv.at[r], (d, s_next))

    msa_copy(0).start()

    pair_in.wait()
    logit_copy.wait_recv()
    gain_copy.wait_recv()
    logits = next_logit[...]
    for r in range(rows):
        normed = standardize(pair_sc[r], next_gain[...]).astype(BF16)
        shard_row = lax.dot_general(
            logits, normed, (((1,), (1,)), ((), ())), preferred_element_type=F32
        )
        for h in range(heads):
            shard[r : r + 1, h * n : (h + 1) * n] = shard_row[h : h + 1, :]

    def shard_copy(index, row, peer):
        return remote(shard, stage.at[row], b_send.at[index], b_recv.at[row], peer)

    shard_copy(0, low, (d, s_next)).start()
    shard_copy(1, low, (other, s_next)).start()
    for r in range(1, rows):
        msa_copy(r).start()
    shard_copy(0, 0, (d, s_next)).wait_recv()
    shard_copy(1, 1, (other, s_next)).wait_recv()
    bias[slot(0, 0)] = jnp.concatenate([stage[0], stage[1]], axis=0).astype(BF16)

    def z_right_copy(t, block):
        return remote(bias.at[block], bias.at[block], zr_send.at[t], zr_recv.at[t], (z_right, s))

    def z_left_copy(t, block):
        return remote(bias.at[block], bias.at[block], zl_send.at[t], zl_recv.at[t], (z_left, s))

    def x_right_copy(t, block):
        return remote(bias.at[block], bias.at[block], xr_send.at[t], xr_recv.at[t], (x_right, s))

    def x_left_copy(t, block):
        return remote(bias.at[block], bias.at[block], xl_send.at[t], xl_recv.at[t], (x_left, s))

    own = slot(0, 0)
    z_right_copy(0, own).start()
    z_left_copy(0, own).start()
    x_right_copy(0, own).start()
    x_left_copy(0, own).start()

    def pass_right(t):
        block = slot(-1, -t)
        x_right_copy(t, block).wait_recv()
        x_right_copy(nz + t - 1, block).start()

    def pass_left(t):
        block = slot(1, t)
        x_left_copy(jnp.where(t == 0, 0, n_right + t), block).wait_recv()
        x_left_copy(nz + t, block).start()

    def gather_step(t, carry):
        block = slot(0, -t)
        z_right_copy(t - 1, block).wait_recv()

        @pl.when(t < n_right)
        def _():
            z_right_copy(t, block).start()

        x_right_copy(t, block).start()
        x_left_copy(t, block).start()

        @pl.when(t <= n_left)
        def _():
            above = slot(0, t)
            z_left_copy(t - 1, above).wait_recv()

            @pl.when(t < n_left)
            def _():
                z_left_copy(t, above).start()

            x_right_copy(n_right + t, above).start()
            x_left_copy(n_right + t, above).start()

        @pl.when(t > 1)
        def _():
            pass_right(t - 1)

        pass_left(t - 1)
        return carry

    lax.fori_loop(1, n_right + 1, gather_step, 0)
    pass_right(n_right)

    def finish(t, carry):
        x_right_copy(jnp.where(t == 0, 0, n_right + t), slot(-1, t)).wait_recv()
        x_left_copy(t + 1, slot(1, -t - 1)).wait_recv()
        x_right_copy(nz + t, slot(-2, -t - 1)).wait_recv()
        x_left_copy(nz + t, slot(2, t)).wait_recv()
        return carry

    lax.fori_loop(0, n_right, finish, 0)

    pair_copy = remote(
        pair_hbm.at[0], pair_out_hbm.at[0], p_send.at[0], p_recv.at[0], (d, s_next)
    )
    pair_copy.start()

    w_in.wait()
    wo_in.wait()
    member = lax.broadcasted_iota(jnp.int32, (n, HALF), 1) // dim
    for h in range(heads):
        v_sc[h * n : (h + 1) * n, HALF:] = jnp.where(member == h % (HALF // dim), 1.0, 0.0).astype(BF16)

    def out_copy(r):
        return pltpu.make_async_copy(x_sc.at[r], out_hbm.at[0, r], local_sem.at[3 + r])

    def row_step(r, carry):
        msa_copy(r).wait_recv()
        x_sc[r] = attend_row(
            x_sc[r],
            bias,
            w_sc,
            wo_sc[...],
            gain_ref[...],
            offset_ref[...],
            out_bias_ref[...],
            (q_sc, k_sc, v_sc, gate_sc, gated_sc),
            heads,
            dim,
        )
        out_copy(r).start()
        return carry

    lax.fori_loop(0, rows, row_step, 0)

    logit_copy.wait_send()
    gain_copy.wait_send()
    shard_copy(0, low, (d, s_next)).wait_send()
    shard_copy(1, low, (other, s_next)).wait_send()

    def drain_z_right(t, carry):
        z_right_copy(t, own).wait_send()
        return carry

    def drain_z_left(t, carry):
        z_left_copy(t, own).wait_send()
        return carry

    def drain_x(t, carry):
        x_right_copy(t, own).wait_send()
        x_left_copy(t, own).wait_send()
        return carry

    def drain_rows(r, carry):
        msa_copy(r).wait_send()
        out_copy(r).wait()
        return carry

    lax.fori_loop(0, n_right, drain_z_right, 0)
    lax.fori_loop(0, n_left, drain_z_left, 0)
    lax.fori_loop(0, nz + n_right, drain_x, 0)
    lax.fori_loop(0, rows, drain_rows, 0)
    pair_copy.wait()


NX, LOW = 4, 2


def body(
    ndap,
    ns,
    msa,
    pair,
    weights,
    w_out,
    logit,
    gain,
    pair_gain,
    offset,
    out_bias,
):
    _, rows, n, width = msa.shape
    pair_width, heads = logit.shape[1:]
    dim = width // heads
    nz = ndap // (NX * LOW)
    n_right, n_left = nz // 2, nz - 1 - nz // 2
    hops = nz + n_right
    hbm = pl.BlockSpec(memory_space=pltpu.HBM)
    vmem = pl.BlockSpec(memory_space=pltpu.VMEM)
    dma = pltpu.SemaphoreType.DMA
    return pl.pallas_call(
        functools.partial(kernel, NX, nz, ns, heads, dim),
        out_shape=(
            jax.ShapeDtypeStruct(msa.shape, F32),
            jax.ShapeDtypeStruct(pair.shape, F32),
        ),
        in_specs=[hbm] * 4 + [vmem] * 5,
        out_specs=(hbm, hbm),
        scratch_shapes=[
            pltpu.VMEM((rows, n, width), F32),
            pltpu.VMEM((rows, n, pair_width), F32),
            pltpu.VMEM((width, 4 * width), BF16),
            pltpu.VMEM((width, width), BF16),
            pltpu.VMEM((heads, pair_width), BF16),
            pltpu.VMEM((1, pair_width), F32),
            pltpu.VMEM((rows, heads * n), F32),
            pltpu.VMEM((2, rows, heads * n), F32),
            pltpu.VMEM((NX * nz, 2 * rows, heads * n), BF16),
            pltpu.VMEM((n, width), BF16),
            pltpu.VMEM((heads * n, HALF), BF16),
            pltpu.VMEM((heads * n, 2 * HALF), BF16),
            pltpu.VMEM((n, width), F32),
            pltpu.VMEM((n, width), BF16),
            dma((3 + rows,)),
            dma((2,)),
            dma((2,)),
            dma((2,)),
            dma((2,)),
            dma((n_right,)),
            dma((n_right,)),
            dma((n_left,)),
            dma((n_left,)),
            dma((hops,)),
            dma((hops,)),
            dma((hops,)),
            dma((hops,)),
            dma((rows,)),
            dma((rows,)),
            dma((1,)),
            dma((1,)),
        ],
        compiler_params=pltpu.CompilerParams(
            collective_id=0, has_side_effects=True, vmem_limit_bytes=48 << 20
        ),
    )(
        msa,
        pair,
        weights,
        w_out,
        logit[0].T,
        gain,
        pair_gain,
        offset,
        out_bias,
    )


def solution(mesh):
    wide = P("section", "dap", None, None)
    flat = P("section", None)
    in_specs = (wide, wide, P("section", None, None), P("section", None, None), P("section", None, None)) + (flat,) * 4
    return jax.shard_map(
        functools.partial(body, mesh.shape["dap"], mesh.shape["section"]),
        mesh=mesh,
        in_specs=in_specs,
        out_specs=(wide, wide),
        check_vma=False,
    )
```

```python
import functools

import jax
import jax.numpy as jnp
from jax import lax
from jax.experimental import pallas as pl
from jax.experimental.pallas import tpu as pltpu
from jax.sharding import PartitionSpec as P

EPSILON = 1e-05
MESH = pl.DeviceIdType.MESH
BF16 = jnp.bfloat16
F32 = jnp.float32
HALF = 128


def whiten(values):
    center = values - jnp.mean(values, axis=-1, keepdims=True)
    spread = jnp.mean(center * center, axis=-1, keepdims=True)
    return center * lax.rsqrt(spread + EPSILON)


def prepare_row(r, x, weights, gain, offset, q_sc, k_sc, v_sc, gate_sc, heads, dim):
    n, width = x.shape
    per_half = HALF // dim
    normed = (whiten(x) * gain).astype(BF16)
    member = lax.broadcasted_iota(jnp.int32, (n, HALF), 1) // dim

    def project(block):
        return jnp.dot(
            normed, weights[:, block * width : (block + 1) * width], preferred_element_type=F32
        )

    q_sc[r] = (project(0) * (1.0 / dim**0.5)).astype(BF16)
    keys = project(1)
    values = project(2)
    for h in range(heads):
        lanes = slice(h // per_half * HALF, (h // per_half + 1) * HALF)
        mine = member == h % per_half
        k_sc[r, h * n : (h + 1) * n, :] = jnp.where(mine, keys[:, lanes], 0.0).astype(BF16)
        v_sc[r, h * n : (h + 1) * n, :HALF] = jnp.where(mine, values[:, lanes], 0.0).astype(BF16)
    gate_sc[r] = jax.nn.sigmoid(project(3) + offset)


def attend_row(r, x, bias, w_out, out_bias, q_sc, k_sc, v_sc, gate_sc, gated_sc, heads, dim):
    n, width = x.shape
    per_half = HALF // dim
    for half in range(width // HALF):
        lanes = slice(half * HALF, (half + 1) * HALF)
        queries = q_sc[r, :, lanes]
        total = None
        for pair in range(per_half // 2):
            h = half * per_half + pair * 2
            scores = lax.dot_general(
                queries,
                k_sc[r, h * n : (h + 2) * n, :],
                (((1,), (1,)), ((), ())),
                preferred_element_type=F32,
            )
            probs = []
            for u in range(2):
                own = bias[:, :, (h + u) * n : (h + u + 1) * n].astype(F32).reshape(n, n)
                shifted = scores[:, u * n : (u + 1) * n] + own
                top = jnp.max(shifted, axis=-1, keepdims=True)
                probs.append(jnp.exp(shifted - top).astype(BF16))
            part = jnp.dot(
                jnp.concatenate(probs, axis=-1),
                v_sc[r, h * n : (h + 2) * n, :],
                preferred_element_type=F32,
            )
            total = part if total is None else total + part
        gated_sc[:, lanes] = (total[:, :HALF] / total[:, HALF:] * gate_sc[r, :, lanes]).astype(BF16)
    return x + (jnp.dot(gated_sc[...], w_out, preferred_element_type=F32) + out_bias)


def kernel(
    nx,
    nz,
    ns,
    heads,
    dim,
    msa_hbm,
    pair_hbm,
    weights_hbm,
    w_out_hbm,
    logit_hbm,
    gain_hbm,
    pair_gain_hbm,
    offset_hbm,
    out_bias_hbm,
    out_hbm,
    pair_out_hbm,
    x_sc,
    pair_sc,
    w_sc,
    wo_sc,
    gain_sc,
    offset_sc,
    out_bias_sc,
    next_logit,
    next_gain,
    shard,
    stage,
    relay,
    bias,
    q_sc,
    k_sc,
    v_sc,
    gate_sc,
    gated_sc,
    local_sem,
    w_send,
    w_recv,
    b_send,
    b_recv,
    zr_send,
    zr_recv,
    zl_send,
    zl_recv,
    xr_send,
    xr_recv,
    xl_send,
    xl_recv,
    m_send,
    m_recv,
    p_send,
    p_recv,
    leg_send,
    leg_recv,
    pass_send,
):
    rows, n = x_sc.shape[0], x_sc.shape[1]
    n_right = nz // 2
    n_left = nz - 1 - n_right
    d = lax.axis_index("dap")
    s = lax.axis_index("section")
    ndap = nx * nz * 2
    x = lax.div(d, 2 * nz)
    z = lax.rem(lax.div(d, 2), nz)
    low = lax.rem(d, 2)
    base = d - 2 * z
    z_right = base + 2 * lax.rem(z + 1, nz)
    z_left = base + 2 * lax.rem(z + nz - 1, nz)
    x_right = lax.rem(d + 2 * nz, ndap)
    x_left = lax.rem(d + ndap - 2 * nz, ndap)
    other = d + 1 - 2 * low
    s_next = lax.rem(s + 1, ns)
    s_prev = lax.rem(s + ns - 1, ns)
    core = lax.rem(s, 2)
    y = 2 * lax.div(s, 2) + low
    y_back = lax.rem(y + ns - 3, ns)
    y_ahead = lax.rem(y + 3, ns)

    def chip(at, on_core):
        return (d - low + lax.rem(at, 2), 2 * lax.div(at, 2) + on_core)

    relay_to = chip(y_back, 1)
    relay_from = chip(y_ahead, 1)
    last_stop = chip(y_back, 0)

    def slot(dx, dz):
        return lax.rem(x + dx + nx, nx) * nz + lax.rem(z + dz + nz, nz)

    pair_in = pltpu.make_async_copy(pair_hbm.at[0], pair_sc, local_sem.at[rows])
    fetched = [
        pltpu.make_async_copy(src, dst, local_sem.at[rows + 1 + i])
        for i, (src, dst) in enumerate(
            (
                (weights_hbm.at[0], w_sc),
                (w_out_hbm.at[0], wo_sc),
                (gain_hbm, gain_sc),
                (offset_hbm, offset_sc),
                (out_bias_hbm, out_bias_sc),
            )
        )
    ]
    pair_in.start()
    for copy in fetched:
        copy.start()

    barrier = pltpu.get_barrier_semaphore()
    peers = (
        (z_right, s),
        (z_left, s),
        (x_right, s),
        (x_left, s),
        (d, s_next),
        (d, s_prev),
        (other, s_next),
        (other, s_prev),
        relay_from,
    )
    for peer in peers:
        pl.semaphore_signal(barrier, inc=1, device_id=peer, device_id_type=MESH)

    @pl.when(core == 1)
    def _():
        pl.semaphore_signal(barrier, inc=1, device_id=relay_to, device_id_type=MESH)
        pl.semaphore_signal(barrier, inc=1, device_id=last_stop, device_id_type=MESH)

    pl.semaphore_wait(barrier, len(peers) + 2 * core)

    def remote(src, dst, send, recv, peer):
        return pltpu.make_async_remote_copy(
            src_ref=src,
            dst_ref=dst,
            send_sem=send,
            recv_sem=recv,
            device_id=peer,
            device_id_type=MESH,
        )

    logit_copy = remote(logit_hbm, next_logit, w_send.at[0], w_recv.at[0], (d, s_prev))
    gain_copy = remote(pair_gain_hbm, next_gain, w_send.at[1], w_recv.at[1], (d, s_prev))
    logit_copy.start()
    gain_copy.start()

    def msa_copy(r):
        return remote(msa_hbm.at[0, r], x_sc.at[r], m_send.at[r], m_recv.at[r], (d, s_next))

    def pair_copy(r):
        return remote(
            pair_hbm.at[0, r], pair_out_hbm.at[0, r], p_send.at[r], p_recv.at[r], (d, s_next)
        )

    def leg_copy(k):
        return remote(
            pair_hbm.at[0, k + 1], relay.at[k], leg_send.at[k], leg_recv.at[k], relay_to
        )

    def pass_copy(k):
        return remote(
            relay.at[k], pair_out_hbm.at[0, k + 1], pass_send.at[k], p_recv.at[k + 1], last_stop
        )

    def relay_step(k):
        @pl.when(core == 1)
        def _():
            leg_copy(k).wait_recv()
            pass_copy(k).start()
            if k + 1 < rows - 1:
                leg_copy(k + 1).start()

    msa_copy(0).start()

    @pl.when(core == 1)
    def _():
        leg_copy(0).start()

    member = lax.broadcasted_iota(jnp.int32, (n, HALF), 1) // dim

    def ones_step(r, carry):
        for h in range(heads):
            mine = member == h % (HALF // dim)
            v_sc[r, h * n : (h + 1) * n, HALF:] = jnp.where(mine, 1.0, 0.0).astype(BF16)
        return carry

    lax.fori_loop(0, rows, ones_step, 0)
    pair_in.wait()
    for r in range(rows):
        pair_sc[r] = whiten(pair_sc[r])
    logit_copy.wait_recv()
    gain_copy.wait_recv()
    logits = next_logit[...]
    for r in range(rows):
        normed = (pair_sc[r] * next_gain[...]).astype(BF16)
        shard_row = lax.dot_general(
            logits, normed, (((1,), (1,)), ((), ())), preferred_element_type=F32
        )
        for h in range(heads):
            shard[r : r + 1, h * n : (h + 1) * n] = shard_row[h : h + 1, :]

    def shard_copy(index, row, peer):
        return remote(shard, stage.at[row], b_send.at[index], b_recv.at[row], peer)

    shard_copy(0, low, (d, s_next)).start()
    shard_copy(1, low, (other, s_next)).start()
    msa_copy(1).start()

    @pl.when(core == 0)
    def _():
        for r in range(2, rows):
            msa_copy(r).start()
        for r in range(rows):
            pair_copy(r).start()

    shard_copy(0, 0, (d, s_next)).wait_recv()
    shard_copy(1, 1, (other, s_next)).wait_recv()
    own = slot(0, 0)
    bias[own] = jnp.concatenate([stage[0], stage[1]], axis=0).astype(BF16)

    def z_right_copy(t, block):
        return remote(bias.at[block], bias.at[block], zr_send.at[t], zr_recv.at[t], (z_right, s))

    def z_left_copy(t, block):
        return remote(bias.at[block], bias.at[block], zl_send.at[t], zl_recv.at[t], (z_left, s))

    def x_right_copy(t, block):
        return remote(bias.at[block], bias.at[block], xr_send.at[t], xr_recv.at[t], (x_right, s))

    def x_left_copy(t, block):
        return remote(bias.at[block], bias.at[block], xl_send.at[t], xl_recv.at[t], (x_left, s))

    z_right_copy(0, own).start()
    z_left_copy(0, own).start()
    x_right_copy(0, own).start()
    x_left_copy(0, own).start()
    relay_step(0)

    def pass_right(t):
        block = slot(-1, -t)
        x_right_copy(t, block).wait_recv()
        x_right_copy(nz + t - 1, block).start()

    def pass_left(t):
        block = slot(1, t)
        x_left_copy(jnp.where(t == 0, 0, n_right + t), block).wait_recv()
        x_left_copy(nz + t, block).start()

    def gather_step(t, carry):
        block = slot(0, -t)
        z_right_copy(t - 1, block).wait_recv()

        @pl.when(t < n_right)
        def _():
            z_right_copy(t, block).start()

        x_right_copy(t, block).start()
        x_left_copy(t, block).start()

        @pl.when(t <= n_left)
        def _():
            above = slot(0, t)
            z_left_copy(t - 1, above).wait_recv()

            @pl.when(t < n_left)
            def _():
                z_left_copy(t, above).start()

            x_right_copy(n_right + t, above).start()
            x_left_copy(n_right + t, above).start()

        @pl.when(t > 1)
        def _():
            pass_right(t - 1)

        pass_left(t - 1)
        for r in range(2, rows):

            @pl.when((t == 3 * r - 4) & (core == 1))
            def _(r=r):
                msa_copy(r - 2).wait_send()
                msa_copy(r).start()

        @pl.when(t == 4)
        def _():
            relay_step(1)

        return carry

    lax.fori_loop(1, n_right + 1, gather_step, 0)
    pass_right(n_right)
    relay_step(2)

    @pl.when(core == 1)
    def _():
        pair_copy(0).start()

    for copy in fetched:
        copy.wait()

    def prepare(r, carry):
        msa_copy(r).wait_recv()
        prepare_row(
            r, x_sc[r], w_sc, gain_sc[...], offset_sc[...], q_sc, k_sc, v_sc, gate_sc, heads, dim
        )
        return carry

    lax.fori_loop(0, rows - 1, prepare, 0)

    def finish(t, carry):
        x_right_copy(jnp.where(t == 0, 0, n_right + t), slot(-1, t)).wait_recv()
        x_left_copy(t + 1, slot(1, -t - 1)).wait_recv()
        x_right_copy(nz + t, slot(-2, -t - 1)).wait_recv()
        x_left_copy(nz + t, slot(2, t)).wait_recv()
        return carry

    lax.fori_loop(0, n_right, finish, 0)

    def out_copy(r):
        return pltpu.make_async_copy(x_sc.at[r], out_hbm.at[0, r], local_sem.at[r])

    def row_step(r, carry):
        @pl.when(r == rows - 1)
        def _():
            prepare(r, 0)

        x_sc[r] = attend_row(
            r,
            x_sc[r],
            bias,
            wo_sc[...],
            out_bias_sc[...],
            q_sc,
            k_sc,
            v_sc,
            gate_sc,
            gated_sc,
            heads,
            dim,
        )
        out_copy(r).start()
        return carry

    lax.fori_loop(0, rows, row_step, 0)

    logit_copy.wait_send()
    gain_copy.wait_send()
    shard_copy(0, low, (d, s_next)).wait_send()
    shard_copy(1, low, (other, s_next)).wait_send()

    def drain_z_right(t, carry):
        z_right_copy(t, own).wait_send()
        return carry

    def drain_z_left(t, carry):
        z_left_copy(t, own).wait_send()
        return carry

    def drain_x(t, carry):
        x_right_copy(t, own).wait_send()
        x_left_copy(t, own).wait_send()
        return carry

    def drain_rows(r, carry):
        @pl.when((core == 0) | (r >= rows - 2))
        def _():
            msa_copy(r).wait_send()

        out_copy(r).wait()
        return carry

    lax.fori_loop(0, n_right, drain_z_right, 0)
    lax.fori_loop(0, n_left, drain_z_left, 0)
    lax.fori_loop(0, nz + n_right, drain_x, 0)
    lax.fori_loop(0, rows, drain_rows, 0)
    pair_copy(0).wait_send()
    for k in range(rows - 1):

        @pl.when(core == 1)
        def _(k=k):
            leg_copy(k).wait_send()
            pass_copy(k).wait_send()

        @pl.when(core == 0)
        def _(k=k):
            pair_copy(k + 1).wait_send()

    for r in range(rows):
        pair_copy(r).wait_recv()


NX, LOW = 4, 2


def body(
    ndap,
    ns,
    msa,
    pair,
    weights,
    w_out,
    logit,
    gain,
    pair_gain,
    offset,
    out_bias,
):
    _, rows, n, width = msa.shape
    pair_width, heads = logit.shape[1:]
    dim = width // heads
    nz = ndap // (NX * LOW)
    n_right, n_left = nz // 2, nz - 1 - nz // 2
    hops = nz + n_right
    hbm = pl.BlockSpec(memory_space=pltpu.HBM)
    dma = pltpu.SemaphoreType.DMA
    return pl.pallas_call(
        functools.partial(kernel, NX, nz, ns, heads, dim),
        out_shape=(
            jax.ShapeDtypeStruct(msa.shape, F32),
            jax.ShapeDtypeStruct(pair.shape, F32),
        ),
        in_specs=[hbm] * 9,
        out_specs=(hbm, hbm),
        scratch_shapes=[
            pltpu.VMEM((rows, n, width), F32),
            pltpu.VMEM((rows, n, pair_width), F32),
            pltpu.VMEM((width, 4 * width), BF16),
            pltpu.VMEM((width, width), BF16),
            pltpu.VMEM((1, width), F32),
            pltpu.VMEM((1, width), F32),
            pltpu.VMEM((1, width), F32),
            pltpu.VMEM((heads, pair_width), BF16),
            pltpu.VMEM((1, pair_width), F32),
            pltpu.VMEM((rows, heads * n), F32),
            pltpu.VMEM((2, rows, heads * n), F32),
            pltpu.VMEM((rows - 1, n, pair_width), F32),
            pltpu.VMEM((NX * nz, 2 * rows, heads * n), BF16),
            pltpu.VMEM((rows, n, width), BF16),
            pltpu.VMEM((rows, heads * n, HALF), BF16),
            pltpu.VMEM((rows, heads * n, 2 * HALF), BF16),
            pltpu.VMEM((rows, n, width), F32),
            pltpu.VMEM((n, width), BF16),
            dma((rows + 6,)),
            dma((2,)),
            dma((2,)),
            dma((2,)),
            dma((2,)),
            dma((n_right,)),
            dma((n_right,)),
            dma((n_left,)),
            dma((n_left,)),
            dma((hops,)),
            dma((hops,)),
            dma((hops,)),
            dma((hops,)),
            dma((rows,)),
            dma((rows,)),
            dma((rows,)),
            dma((rows,)),
            dma((rows - 1,)),
            dma((rows - 1,)),
            dma((rows - 1,)),
        ],
        compiler_params=pltpu.CompilerParams(
            collective_id=0, has_side_effects=True, vmem_limit_bytes=60 << 20
        ),
    )(
        msa,
        pair,
        weights,
        w_out,
        logit[0].T,
        gain,
        pair_gain,
        offset,
        out_bias,
    )


def solution(mesh):
    wide = P("section", "dap", None, None)
    deep = P("section", None, None)
    flat = P("section", None)
    return jax.shard_map(
        functools.partial(body, mesh.shape["dap"], mesh.shape["section"]),
        mesh=mesh,
        in_specs=(wide, wide, deep, deep, deep, flat, flat, flat, flat),
        out_specs=(wide, wide),
        check_vma=False,
    )
```

```python
import functools

import jax
import jax.numpy as jnp
from jax import lax
from jax.experimental import pallas as pl
from jax.experimental.pallas import tpu as pltpu
from jax.sharding import PartitionSpec as P

EPSILON = 1e-05
MESH = pl.DeviceIdType.MESH
BF16 = jnp.bfloat16
F32 = jnp.float32
HALF = 128


def whiten(values):
    center = values - jnp.mean(values, axis=-1, keepdims=True)
    spread = jnp.mean(center * center, axis=-1, keepdims=True)
    return center * lax.rsqrt(spread + EPSILON)


def prepare_row(r, x, weights, gain, offset, q_sc, k_sc, v_sc, gate_sc, heads, dim):
    n, width = x.shape
    per_half = HALF // dim
    normed = (whiten(x) * gain).astype(BF16)
    member = lax.broadcasted_iota(jnp.int32, (n, HALF), 1) // dim

    def project(block):
        return jnp.dot(
            normed, weights[:, block * width : (block + 1) * width], preferred_element_type=F32
        )

    q_sc[r] = (project(0) * (1.0 / dim**0.5)).astype(BF16)
    keys = project(1)
    values = project(2)
    for h in range(heads):
        lanes = slice(h // per_half * HALF, (h // per_half + 1) * HALF)
        mine = member == h % per_half
        k_sc[r, h * n : (h + 1) * n, :] = jnp.where(mine, keys[:, lanes], 0.0).astype(BF16)
        v_sc[r, h * n : (h + 1) * n, :HALF] = jnp.where(mine, values[:, lanes], 0.0).astype(BF16)
    gate_sc[r] = jax.nn.sigmoid(project(3) + offset)


def attend_row(r, x, bias, w_out, out_bias, q_sc, k_sc, v_sc, gate_sc, gated_sc, heads, dim):
    n, width = x.shape
    per_half = HALF // dim
    for half in range(width // HALF):
        lanes = slice(half * HALF, (half + 1) * HALF)
        queries = q_sc[r, :, lanes]
        total = None
        for pair in range(per_half // 2):
            h = half * per_half + pair * 2
            scores = lax.dot_general(
                queries,
                k_sc[r, h * n : (h + 2) * n, :],
                (((1,), (1,)), ((), ())),
                preferred_element_type=F32,
            )
            probs = []
            for u in range(2):
                own = bias[:, :, (h + u) * n : (h + u + 1) * n].astype(F32).reshape(n, n)
                shifted = scores[:, u * n : (u + 1) * n] + own
                top = jnp.max(shifted, axis=-1, keepdims=True)
                probs.append(jnp.exp(shifted - top).astype(BF16))
            part = jnp.dot(
                jnp.concatenate(probs, axis=-1),
                v_sc[r, h * n : (h + 2) * n, :],
                preferred_element_type=F32,
            )
            total = part if total is None else total + part
        gated_sc[:, lanes] = (total[:, :HALF] / total[:, HALF:] * gate_sc[r, :, lanes]).astype(BF16)
    return x + (jnp.dot(gated_sc[...], w_out, preferred_element_type=F32) + out_bias)


def kernel(
    nx,
    nz,
    ns,
    heads,
    dim,
    msa_hbm,
    pair_hbm,
    weights_hbm,
    w_out_hbm,
    logit_hbm,
    gain_hbm,
    pair_gain_hbm,
    offset_hbm,
    out_bias_hbm,
    out_hbm,
    pair_out_hbm,
    x_sc,
    pair_sc,
    w_sc,
    wo_sc,
    gain_sc,
    offset_sc,
    out_bias_sc,
    next_logit,
    next_gain,
    shard,
    shard_half,
    stage,
    relay,
    bias,
    q_sc,
    k_sc,
    v_sc,
    gate_sc,
    gated_sc,
    local_sem,
    w_send,
    w_recv,
    b_send,
    b_recv,
    zr_send,
    zr_recv,
    zl_send,
    zl_recv,
    xr_send,
    xr_recv,
    xl_send,
    xl_recv,
    far_send,
    far_recv,
    fr_send,
    fr_recv,
    fl_send,
    fl_recv,
    m_send,
    m_recv,
    p_send,
    p_recv,
    leg_send,
    leg_recv,
    pass_send,
):
    rows, n = x_sc.shape[0], x_sc.shape[1]
    n_right = nz // 2
    n_left = nz - 1 - n_right
    d = lax.axis_index("dap")
    s = lax.axis_index("section")
    ndap = nx * nz * 2
    x = lax.div(d, 2 * nz)
    z = lax.rem(lax.div(d, 2), nz)
    low = lax.rem(d, 2)
    base = d - 2 * z
    z_right = base + 2 * lax.rem(z + 1, nz)
    z_left = base + 2 * lax.rem(z + nz - 1, nz)
    x_right = lax.rem(d + 2 * nz, ndap)
    x_left = lax.rem(d + ndap - 2 * nz, ndap)
    x_far = lax.rem(d + 4 * nz, ndap)
    other = d + 1 - 2 * low
    s_next = lax.rem(s + 1, ns)
    s_prev = lax.rem(s + ns - 1, ns)
    core = lax.rem(s, 2)
    y = 2 * lax.div(s, 2) + low
    y_back = lax.rem(y + ns - 3, ns)
    y_ahead = lax.rem(y + 3, ns)

    def chip(at, on_core):
        return (d - low + lax.rem(at, 2), 2 * lax.div(at, 2) + on_core)

    relay_to = chip(y_back, 1)
    relay_from = chip(y_ahead, 1)
    last_stop = chip(y_back, 0)

    def slot(dx, dz):
        return lax.rem(x + dx + nx, nx) * nz + lax.rem(z + dz + nz, nz)

    pair_in = pltpu.make_async_copy(pair_hbm.at[0], pair_sc, local_sem.at[rows])
    fetched = [
        pltpu.make_async_copy(src, dst, local_sem.at[rows + 1 + i])
        for i, (src, dst) in enumerate(
            (
                (weights_hbm.at[0], w_sc),
                (w_out_hbm.at[0], wo_sc),
                (gain_hbm, gain_sc),
                (offset_hbm, offset_sc),
                (out_bias_hbm, out_bias_sc),
            )
        )
    ]
    pair_in.start()
    for copy in fetched:
        copy.start()

    barrier = pltpu.get_barrier_semaphore()
    peers = (
        (z_right, s),
        (z_left, s),
        (x_right, s),
        (x_left, s),
        (x_far, s),
        (d, s_next),
        (d, s_prev),
        (other, s_next),
        (other, s_prev),
        relay_from,
    )
    for peer in peers:
        pl.semaphore_signal(barrier, inc=1, device_id=peer, device_id_type=MESH)

    @pl.when(core == 1)
    def _():
        pl.semaphore_signal(barrier, inc=1, device_id=relay_to, device_id_type=MESH)
        pl.semaphore_signal(barrier, inc=1, device_id=last_stop, device_id_type=MESH)

    pl.semaphore_wait(barrier, len(peers) + 2 * core)

    def remote(src, dst, send, recv, peer):
        return pltpu.make_async_remote_copy(
            src_ref=src,
            dst_ref=dst,
            send_sem=send,
            recv_sem=recv,
            device_id=peer,
            device_id_type=MESH,
        )

    logit_copy = remote(logit_hbm, next_logit, w_send.at[0], w_recv.at[0], (d, s_prev))
    gain_copy = remote(pair_gain_hbm, next_gain, w_send.at[1], w_recv.at[1], (d, s_prev))
    logit_copy.start()
    gain_copy.start()

    def msa_copy(r):
        return remote(msa_hbm.at[0, r], x_sc.at[r], m_send.at[r], m_recv.at[r], (d, s_next))

    def head_copy(half):
        part = pl.ds(half * (n // 2), n // 2)
        return remote(
            msa_hbm.at[0, 0, part],
            x_sc.at[0, part],
            m_send.at[half * rows],
            m_recv.at[half * rows],
            (d, s_next),
        )

    def pair_copy(r):
        return remote(
            pair_hbm.at[0, r], pair_out_hbm.at[0, r], p_send.at[r], p_recv.at[r], (d, s_next)
        )

    def leg_copy(k):
        return remote(
            pair_hbm.at[0, k + 1], relay.at[k], leg_send.at[k], leg_recv.at[k], relay_to
        )

    def pass_copy(k):
        return remote(
            relay.at[k], pair_out_hbm.at[0, k + 1], pass_send.at[k], p_recv.at[k + 1], last_stop
        )

    def relay_step(k):
        @pl.when(core == 1)
        def _():
            leg_copy(k).wait_recv()
            pass_copy(k).start()
            if k + 2 < rows - 1:
                leg_copy(k + 2).start()

    head_copy(0).start()
    member = lax.broadcasted_iota(jnp.int32, (n, HALF), 1) // dim

    def ones_step(r, carry):
        for h in range(heads):
            mine = member == h % (HALF // dim)
            v_sc[r, h * n : (h + 1) * n, HALF:] = jnp.where(mine, 1.0, 0.0).astype(BF16)
        return carry

    lax.fori_loop(0, rows, ones_step, 0)
    pair_in.wait()
    for r in range(rows):
        pair_sc[r] = whiten(pair_sc[r])
    logit_copy.wait_recv()
    gain_copy.wait_recv()

    @pl.when(core == 1)
    def _():
        leg_copy(0).start()
        leg_copy(1).start()

    logits = next_logit[...]
    for r in range(rows):
        normed = (pair_sc[r] * next_gain[...]).astype(BF16)
        shard_row = lax.dot_general(
            logits, normed, (((1,), (1,)), ((), ())), preferred_element_type=F32
        )
        for h in range(heads):
            shard[r : r + 1, h * n : (h + 1) * n] = shard_row[h : h + 1, :]

    shard_half[...] = shard[...].astype(BF16)

    def shard_copy(index, row, peer):
        return remote(shard_half, stage.at[row], b_send.at[index], b_recv.at[row], peer)

    shard_copy(0, low, (d, s_next)).start()
    shard_copy(1, low, (other, s_next)).start()
    head_copy(1).start()
    msa_copy(1).start()
    msa_copy(2).start()

    @pl.when(core == 0)
    def _():
        msa_copy(3).start()
        for r in range(rows):
            pair_copy(r).start()

    shard_copy(0, 0, (d, s_next)).wait_recv()
    shard_copy(1, 1, (other, s_next)).wait_recv()
    own = slot(0, 0)
    bias[own] = jnp.concatenate([stage[0].astype(F32), stage[1].astype(F32)], axis=0).astype(BF16)

    def block_copy(send, recv, t, block, peer):
        return remote(bias.at[block], bias.at[block], send.at[t], recv.at[t], (peer, s))

    def z_right_copy(t, block):
        return block_copy(zr_send, zr_recv, t, block, z_right)

    def z_left_copy(t, block):
        return block_copy(zl_send, zl_recv, t, block, z_left)

    def x_right_copy(t, block):
        return block_copy(xr_send, xr_recv, t, block, x_right)

    def x_left_copy(t, block):
        return block_copy(xl_send, xl_recv, t, block, x_left)

    def far_copy(block):
        return block_copy(far_send, far_recv, 0, block, x_far)

    def far_right_copy(t, block):
        return block_copy(fr_send, fr_recv, t, block, z_right)

    def far_left_copy(t, block):
        return block_copy(fl_send, fl_recv, t, block, z_left)

    far_copy(own).start()
    z_right_copy(0, own).start()
    z_left_copy(0, own).start()
    x_right_copy(0, own).start()
    x_left_copy(0, own).start()

    def far_step(t):
        below = slot(2, -t)
        far_right_copy(t - 1, below).wait_recv()

        @pl.when(t < n_right)
        def _():
            far_right_copy(t, below).start()

        @pl.when(t <= n_left)
        def _():
            above = slot(2, t)
            far_left_copy(t - 1, above).wait_recv()

            @pl.when(t < n_left)
            def _():
                far_left_copy(t, above).start()

    def gather_step(t, carry):
        block = slot(0, -t)
        z_right_copy(t - 1, block).wait_recv()

        @pl.when(t < n_right)
        def _():
            z_right_copy(t, block).start()

        x_right_copy(t, block).start()
        x_left_copy(t, block).start()

        @pl.when(t <= n_left)
        def _():
            above = slot(0, t)
            z_left_copy(t - 1, above).wait_recv()

            @pl.when(t < n_left)
            def _():
                z_left_copy(t, above).start()

            x_right_copy(n_right + t, above).start()
            x_left_copy(n_right + t, above).start()

        @pl.when(t == 1)
        def _():
            far = slot(2, 0)
            far_copy(far).wait_recv()
            far_right_copy(0, far).start()
            far_left_copy(0, far).start()

        @pl.when(t > 1)
        def _():
            far_step(t - 1)

        @pl.when(t == 1)
        def _():
            relay_step(0)

        @pl.when((t == 2) & (core == 1))
        def _():
            msa_copy(3).start()

        @pl.when(t == 4)
        def _():
            relay_step(1)

        return carry

    lax.fori_loop(1, n_right + 1, gather_step, 0)
    far_step(n_right)
    relay_step(2)

    @pl.when(core == 1)
    def _():
        pair_copy(0).start()

    for copy in fetched:
        copy.wait()

    def prepare(r, carry):
        @pl.when(r == 0)
        def _():
            head_copy(0).wait_recv()
            head_copy(1).wait_recv()

        @pl.when(r > 0)
        def _():
            msa_copy(r).wait_recv()

        prepare_row(
            r, x_sc[r], w_sc, gain_sc[...], offset_sc[...], q_sc, k_sc, v_sc, gate_sc, heads, dim
        )
        return carry

    lax.fori_loop(0, rows - 1, prepare, 0)

    def finish(t, carry):
        below, above = jnp.where(t > n_right, 0, t), jnp.where(t > n_right, t - n_right, 0)
        x_right_copy(t, slot(-1, above - below)).wait_recv()
        x_left_copy(t, slot(1, above - below)).wait_recv()
        return carry

    lax.fori_loop(0, nz, finish, 0)

    def out_copy(r):
        return pltpu.make_async_copy(x_sc.at[r], out_hbm.at[0, r], local_sem.at[r])

    def row_step(r, carry):
        @pl.when(r == rows - 1)
        def _():
            prepare(r, 0)

        x_sc[r] = attend_row(
            r,
            x_sc[r],
            bias,
            wo_sc[...],
            out_bias_sc[...],
            q_sc,
            k_sc,
            v_sc,
            gate_sc,
            gated_sc,
            heads,
            dim,
        )
        out_copy(r).start()
        return carry

    lax.fori_loop(0, rows, row_step, 0)

    logit_copy.wait_send()
    gain_copy.wait_send()
    shard_copy(0, low, (d, s_next)).wait_send()
    shard_copy(1, low, (other, s_next)).wait_send()

    def drain_z_right(t, carry):
        z_right_copy(t, own).wait_send()
        far_right_copy(t, own).wait_send()
        return carry

    def drain_z_left(t, carry):
        z_left_copy(t, own).wait_send()
        far_left_copy(t, own).wait_send()
        return carry

    def drain_x(t, carry):
        x_right_copy(t, own).wait_send()
        x_left_copy(t, own).wait_send()
        return carry

    def drain_rows(r, carry):
        @pl.when(r > 0)
        def _():
            msa_copy(r).wait_send()

        out_copy(r).wait()
        return carry

    lax.fori_loop(0, n_right, drain_z_right, 0)
    lax.fori_loop(0, n_left, drain_z_left, 0)
    lax.fori_loop(0, nz, drain_x, 0)
    far_copy(own).wait_send()
    lax.fori_loop(0, rows, drain_rows, 0)
    head_copy(0).wait_send()
    head_copy(1).wait_send()
    pair_copy(0).wait_send()
    for k in range(rows - 1):

        @pl.when(core == 1)
        def _(k=k):
            leg_copy(k).wait_send()
            pass_copy(k).wait_send()

        @pl.when(core == 0)
        def _(k=k):
            pair_copy(k + 1).wait_send()

    for r in range(rows):
        pair_copy(r).wait_recv()


NX, LOW = 4, 2


def body(
    ndap,
    ns,
    msa,
    pair,
    weights,
    w_out,
    logit,
    gain,
    pair_gain,
    offset,
    out_bias,
):
    _, rows, n, width = msa.shape
    pair_width, heads = logit.shape[1:]
    dim = width // heads
    nz = ndap // (NX * LOW)
    n_right, n_left = nz // 2, nz - 1 - nz // 2
    hbm = pl.BlockSpec(memory_space=pltpu.HBM)
    dma = pltpu.SemaphoreType.DMA
    operands = (msa, pair, weights, w_out, logit[0].T, gain, pair_gain, offset, out_bias)
    return pl.pallas_call(
        functools.partial(kernel, NX, nz, ns, heads, dim),
        out_shape=(
            jax.ShapeDtypeStruct(msa.shape, F32),
            jax.ShapeDtypeStruct(pair.shape, F32),
        ),
        in_specs=[hbm] * 9,
        out_specs=(hbm, hbm),
        scratch_shapes=[
            pltpu.VMEM((rows, n, width), F32),
            pltpu.VMEM((rows, n, pair_width), F32),
            pltpu.VMEM((width, 4 * width), BF16),
            pltpu.VMEM((width, width), BF16),
            pltpu.VMEM((1, width), F32),
            pltpu.VMEM((1, width), F32),
            pltpu.VMEM((1, width), F32),
            pltpu.VMEM((heads, pair_width), BF16),
            pltpu.VMEM((1, pair_width), F32),
            pltpu.VMEM((rows, heads * n), F32),
            pltpu.VMEM((rows, heads * n), BF16),
            pltpu.VMEM((2, rows, heads * n), BF16),
            pltpu.VMEM((rows - 1, n, pair_width), F32),
            pltpu.VMEM((NX * nz, 2 * rows, heads * n), BF16),
            pltpu.VMEM((rows, n, width), BF16),
            pltpu.VMEM((rows, heads * n, HALF), BF16),
            pltpu.VMEM((rows, heads * n, 2 * HALF), BF16),
            pltpu.VMEM((rows, n, width), F32),
            pltpu.VMEM((n, width), BF16),
            dma((rows + 6,)),
            dma((2,)),
            dma((2,)),
            dma((2,)),
            dma((2,)),
            dma((n_right,)),
            dma((n_right,)),
            dma((n_left,)),
            dma((n_left,)),
            dma((nz,)),
            dma((nz,)),
            dma((nz,)),
            dma((nz,)),
            dma((1,)),
            dma((1,)),
            dma((n_right,)),
            dma((n_right,)),
            dma((n_left,)),
            dma((n_left,)),
            dma((rows + 1,)),
            dma((rows + 1,)),
            dma((rows,)),
            dma((rows,)),
            dma((rows - 1,)),
            dma((rows - 1,)),
            dma((rows - 1,)),
        ],
        compiler_params=pltpu.CompilerParams(
            collective_id=0, has_side_effects=True, vmem_limit_bytes=44 << 20
        ),
    )(*(pltpu.with_memory_space_constraint(operand, pltpu.HBM) for operand in operands))


def solution(mesh):
    wide = P("section", "dap", None, None)
    deep = P("section", None, None)
    flat = P("section", None)
    return jax.shard_map(
        functools.partial(body, mesh.shape["dap"], mesh.shape["section"]),
        mesh=mesh,
        in_specs=(wide, wide, deep, deep, deep, flat, flat, flat, flat),
        out_specs=(wide, wide),
        check_vma=False,
    )
```

```python
import functools

import jax
import jax.numpy as jnp
from jax import lax
from jax.experimental import pallas as pl
from jax.experimental.pallas import tpu as pltpu
from jax.sharding import PartitionSpec as P

EPSILON = 1e-05
MESH = pl.DeviceIdType.MESH
BF16 = jnp.bfloat16
F32 = jnp.float32
HALF = 128


def whiten(values):
    center = values - jnp.mean(values, axis=-1, keepdims=True)
    spread = jnp.mean(center * center, axis=-1, keepdims=True)
    return center * lax.rsqrt(spread + EPSILON)


def prepare_row(r, x, weights, gain, offset, q_sc, k_sc, v_sc, gate_sc, heads, dim):
    n, width = x.shape
    per_half = HALF // dim
    normed = (whiten(x) * gain).astype(BF16)
    member = lax.broadcasted_iota(jnp.int32, (n, HALF), 1) // dim

    def project(block):
        return jnp.dot(
            normed, weights[:, block * width : (block + 1) * width], preferred_element_type=F32
        )

    q_sc[r] = (project(0) * (1.0 / dim**0.5)).astype(BF16)
    keys = project(1)
    values = project(2)
    for h in range(heads):
        lanes = slice(h // per_half * HALF, (h // per_half + 1) * HALF)
        mine = member == h % per_half
        k_sc[r, h * n : (h + 1) * n, :] = jnp.where(mine, keys[:, lanes], 0.0).astype(BF16)
        v_sc[r, h * n : (h + 1) * n, :HALF] = jnp.where(mine, values[:, lanes], 0.0).astype(BF16)
    gate_sc[r] = jax.nn.sigmoid(project(3) + offset)


def attend_row(r, x, bias, w_out, out_bias, q_sc, k_sc, v_sc, gate_sc, gated_sc, heads, dim):
    n, width = x.shape
    per_half = HALF // dim
    for half in range(width // HALF):
        lanes = slice(half * HALF, (half + 1) * HALF)
        queries = q_sc[r, :, lanes]
        total = None
        for pair in range(per_half // 2):
            h = half * per_half + pair * 2
            scores = lax.dot_general(
                queries,
                k_sc[r, h * n : (h + 2) * n, :],
                (((1,), (1,)), ((), ())),
                preferred_element_type=F32,
            )
            probs = []
            for u in range(2):
                own = bias[:, :, (h + u) * n : (h + u + 1) * n].astype(F32).reshape(n, n)
                shifted = scores[:, u * n : (u + 1) * n] + own
                top = jnp.max(shifted, axis=-1, keepdims=True)
                probs.append(jnp.exp(shifted - top).astype(BF16))
            part = jnp.dot(
                jnp.concatenate(probs, axis=-1),
                v_sc[r, h * n : (h + 2) * n, :],
                preferred_element_type=F32,
            )
            total = part if total is None else total + part
        gated_sc[:, lanes] = (total[:, :HALF] / total[:, HALF:] * gate_sc[r, :, lanes]).astype(BF16)
    return x + (jnp.dot(gated_sc[...], w_out, preferred_element_type=F32) + out_bias)


def kernel(
    nx,
    nz,
    ns,
    heads,
    dim,
    msa_hbm,
    pair_hbm,
    weights_hbm,
    w_out_hbm,
    logit_hbm,
    gain_hbm,
    pair_gain_hbm,
    offset_hbm,
    out_bias_hbm,
    out_hbm,
    pair_out_hbm,
    x_sc,
    pair_sc,
    w_sc,
    wo_sc,
    gain_sc,
    offset_sc,
    out_bias_sc,
    next_logit,
    next_gain,
    shard,
    shard_half,
    stage,
    relay,
    bias,
    q_sc,
    k_sc,
    v_sc,
    gate_sc,
    gated_sc,
    local_sem,
    w_send,
    w_recv,
    b_send,
    b_recv,
    zr_send,
    zr_recv,
    zl_send,
    zl_recv,
    xr_send,
    xr_recv,
    xl_send,
    xl_recv,
    far_send,
    far_recv,
    fr_send,
    fr_recv,
    fl_send,
    fl_recv,
    m_send,
    m_recv,
    p_send,
    p_recv,
    leg_send,
    leg_recv,
    pass_send,
    entered,
):
    rows, n = x_sc.shape[0], x_sc.shape[1]
    n_right = nz // 2
    n_left = nz - 1 - n_right
    d = lax.axis_index("dap")
    s = lax.axis_index("section")
    ndap = nx * nz * 2
    x = lax.div(d, 2 * nz)
    z = lax.rem(lax.div(d, 2), nz)
    low = lax.rem(d, 2)
    base = d - 2 * z
    z_right = base + 2 * lax.rem(z + 1, nz)
    z_left = base + 2 * lax.rem(z + nz - 1, nz)
    z_right2 = base + 2 * lax.rem(z + 2, nz)
    z_left2 = base + 2 * lax.rem(z + nz - 2, nz)
    x_right = lax.rem(d + 2 * nz, ndap)
    x_left = lax.rem(d + ndap - 2 * nz, ndap)
    x_far = lax.rem(d + 4 * nz, ndap)
    other = d + 1 - 2 * low
    s_next = lax.rem(s + 1, ns)
    s_prev = lax.rem(s + ns - 1, ns)
    core = lax.rem(s, 2)
    y = 2 * lax.div(s, 2) + low
    y_back = lax.rem(y + ns - 3, ns)
    y_ahead = lax.rem(y + 3, ns)

    def chip(at, on_core):
        return (d - low + lax.rem(at, 2), 2 * lax.div(at, 2) + on_core)

    relay_to = chip(y_back, 1)
    relay_from = chip(y_ahead, 1)
    last_stop = chip(y_back, 0)

    def slot(dx, dz):
        return lax.rem(x + dx + nx, nx) * nz + lax.rem(z + dz + nz, nz)

    pair_in = pltpu.make_async_copy(pair_hbm.at[0], pair_sc, local_sem.at[rows])
    fetched = [
        pltpu.make_async_copy(src, dst, local_sem.at[rows + 1 + i])
        for i, (src, dst) in enumerate(
            (
                (weights_hbm.at[0], w_sc),
                (w_out_hbm.at[0], wo_sc),
                (gain_hbm, gain_sc),
                (offset_hbm, offset_sc),
                (out_bias_hbm, out_bias_sc),
            )
        )
    ]
    pair_in.start()
    for copy in fetched:
        copy.start()

    barrier = pltpu.get_barrier_semaphore()
    peers = (
        (x_right, s),
        (x_left, s),
        (x_far, s),
        (d, s_next),
        (d, s_prev),
        (other, s_next),
        (other, s_prev),
        relay_from,
    )
    for peer in peers:
        pl.semaphore_signal(barrier, inc=1, device_id=peer, device_id_type=MESH)

    @pl.when(core == 1)
    def _():
        pl.semaphore_signal(barrier, inc=1, device_id=relay_to, device_id_type=MESH)
        pl.semaphore_signal(barrier, inc=1, device_id=last_stop, device_id_type=MESH)

    along = (
        (z_right, z == nz - 1, 2),
        (z_right2, z >= nz - 2, 3),
        (z_left, z >= 1, 0),
        (z_left2, z >= 2, 1),
    )
    expected = len(peers) + 2 * core
    for peer, smaller, _ in along:
        expected = expected + jnp.where(smaller, 1, 0)

        @pl.when(jnp.logical_not(smaller))
        def _(peer=peer):
            pl.semaphore_signal(barrier, inc=1, device_id=(peer, s), device_id_type=MESH)

    pl.semaphore_wait(barrier, expected)
    for peer, smaller, mark in along:

        @pl.when(smaller)
        def _(peer=peer, mark=mark):
            pl.semaphore_signal(
                entered.at[mark], inc=1, device_id=(peer, s), device_id_type=MESH
            )

    def await_entry(index):
        @pl.when(jnp.logical_not(along[index][1]))
        def _():
            pl.semaphore_wait(entered.at[index], 1)

    def remote(src, dst, send, recv, peer):
        return pltpu.make_async_remote_copy(
            src_ref=src,
            dst_ref=dst,
            send_sem=send,
            recv_sem=recv,
            device_id=peer,
            device_id_type=MESH,
        )

    logit_copy = remote(logit_hbm, next_logit, w_send.at[0], w_recv.at[0], (d, s_prev))
    gain_copy = remote(pair_gain_hbm, next_gain, w_send.at[1], w_recv.at[1], (d, s_prev))
    logit_copy.start()
    gain_copy.start()

    def msa_copy(r):
        return remote(msa_hbm.at[0, r], x_sc.at[r], m_send.at[r], m_recv.at[r], (d, s_next))

    def head_copy(half):
        part = pl.ds(half * (n // 2), n // 2)
        return remote(
            msa_hbm.at[0, 0, part],
            x_sc.at[0, part],
            m_send.at[half * rows],
            m_recv.at[half * rows],
            (d, s_next),
        )

    def pair_copy(r):
        return remote(
            pair_hbm.at[0, r], pair_out_hbm.at[0, r], p_send.at[r], p_recv.at[r], (d, s_next)
        )

    def leg_copy(k):
        return remote(
            pair_hbm.at[0, k + 1], relay.at[k], leg_send.at[k], leg_recv.at[k], relay_to
        )

    def pass_copy(k):
        return remote(
            relay.at[k], pair_out_hbm.at[0, k + 1], pass_send.at[k], p_recv.at[k + 1], last_stop
        )

    def relay_step(k):
        @pl.when(core == 1)
        def _():
            leg_copy(k).wait_recv()
            pass_copy(k).start()
            if k + 2 < rows - 1:
                leg_copy(k + 2).start()

    head_copy(0).start()
    member = lax.broadcasted_iota(jnp.int32, (n, HALF), 1) // dim

    def ones_step(r, carry):
        for h in range(heads):
            mine = member == h % (HALF // dim)
            v_sc[r, h * n : (h + 1) * n, HALF:] = jnp.where(mine, 1.0, 0.0).astype(BF16)
        return carry

    lax.fori_loop(0, rows, ones_step, 0)
    pair_in.wait()
    for r in range(rows):
        pair_sc[r] = whiten(pair_sc[r])
    logit_copy.wait_recv()
    gain_copy.wait_recv()

    @pl.when(core == 1)
    def _():
        leg_copy(0).start()
        leg_copy(1).start()

    logits = next_logit[...]
    for r in range(rows):
        normed = (pair_sc[r] * next_gain[...]).astype(BF16)
        shard_row = lax.dot_general(
            logits, normed, (((1,), (1,)), ((), ())), preferred_element_type=F32
        )
        for h in range(heads):
            shard[r : r + 1, h * n : (h + 1) * n] = shard_row[h : h + 1, :]

    shard_half[...] = shard[...].astype(BF16)

    def shard_copy(index, row, peer):
        return remote(shard_half, stage.at[row], b_send.at[index], b_recv.at[row], peer)

    shard_copy(0, low, (d, s_next)).start()
    shard_copy(1, low, (other, s_next)).start()
    head_copy(1).start()
    msa_copy(1).start()
    msa_copy(2).start()

    @pl.when(core == 0)
    def _():
        msa_copy(3).start()
        for r in range(rows):
            pair_copy(r).start()

    shard_copy(0, 0, (d, s_next)).wait_recv()
    shard_copy(1, 1, (other, s_next)).wait_recv()
    own = slot(0, 0)
    bias[own] = jnp.concatenate([stage[0].astype(F32), stage[1].astype(F32)], axis=0).astype(BF16)

    def block_copy(send, recv, t, block, peer):
        return remote(bias.at[block], bias.at[block], send.at[t], recv.at[t], (peer, s))

    def z_right_copy(t, block):
        return block_copy(zr_send, zr_recv, t - 1, block, z_right if t % 2 else z_right2)

    def z_left_copy(t, block):
        return block_copy(zl_send, zl_recv, t - 1, block, z_left if t % 2 else z_left2)

    def x_right_copy(t, block):
        return block_copy(xr_send, xr_recv, t, block, x_right)

    def x_left_copy(t, block):
        return block_copy(xl_send, xl_recv, t, block, x_left)

    def far_copy(block):
        return block_copy(far_send, far_recv, 0, block, x_far)

    def far_right_copy(t, block):
        return block_copy(fr_send, fr_recv, t - 1, block, z_right if t % 2 else z_right2)

    def far_left_copy(t, block):
        return block_copy(fl_send, fl_recv, t - 1, block, z_left if t % 2 else z_left2)

    def send_on(right, left, at, below, above):
        for t in (at + 2, at + 1):
            if t <= n_right and below is not None:
                right(t, below).start()
            if t <= n_left and above is not None:
                left(t, above).start()

    def beside(index, block):
        x_right_copy(index, block).start()
        x_left_copy(index, block).start()

    far_copy(own).start()
    beside(0, own)
    await_entry(0)
    await_entry(1)
    send_on(z_right_copy, z_left_copy, 0, own, None)
    await_entry(2)
    await_entry(3)
    send_on(z_right_copy, z_left_copy, 0, None, own)

    def far_round(at):
        for t in (at + 2, at + 1):
            if t <= n_right:
                far_right_copy(t, slot(2, -t)).wait_recv()
                if t % 2 == 0:
                    send_on(far_right_copy, far_left_copy, t, slot(2, -t), None)
            if t <= n_left:
                far_left_copy(t, slot(2, t)).wait_recv()
                if t % 2 == 0:
                    send_on(far_right_copy, far_left_copy, t, None, slot(2, t))

    def near_round(at):
        for t in (at + 2, at + 1):
            if t <= n_right:
                z_right_copy(t, slot(0, -t)).wait_recv()
                if t % 2 == 0:
                    send_on(z_right_copy, z_left_copy, t, slot(0, -t), None)
                beside(t, slot(0, -t))
            if t <= n_left:
                z_left_copy(t, slot(0, t)).wait_recv()
                if t % 2 == 0:
                    send_on(z_right_copy, z_left_copy, t, None, slot(0, t))
                beside(n_right + t, slot(0, t))

    last = (n_right - 1) // 2 * 2
    for at in range(0, last + 1, 2):
        near_round(at)
        if at == 0:
            far = slot(2, 0)
            far_copy(far).wait_recv()
            send_on(far_right_copy, far_left_copy, 0, far, far)

            @pl.when(core == 1)
            def _():
                msa_copy(3).start()

        else:
            far_round(at - 2)
            relay_step(at // 2 - 1)
    far_round(last)
    @pl.when(core == 1)
    def _():
        pair_copy(0).start()

    for copy in fetched:
        copy.wait()

    def prepare(r, carry):
        @pl.when(r == 0)
        def _():
            head_copy(0).wait_recv()
            head_copy(1).wait_recv()

        @pl.when(r > 0)
        def _():
            msa_copy(r).wait_recv()

        prepare_row(
            r, x_sc[r], w_sc, gain_sc[...], offset_sc[...], q_sc, k_sc, v_sc, gate_sc, heads, dim
        )
        return carry

    lax.fori_loop(0, rows - 1, prepare, 0)
    relay_step(2)

    def finish(t, carry):
        below, above = jnp.where(t > n_right, 0, t), jnp.where(t > n_right, t - n_right, 0)
        x_right_copy(t, slot(-1, above - below)).wait_recv()
        x_left_copy(t, slot(1, above - below)).wait_recv()
        return carry

    lax.fori_loop(0, nz, finish, 0)

    def out_copy(r):
        return pltpu.make_async_copy(x_sc.at[r], out_hbm.at[0, r], local_sem.at[r])

    def row_step(r, carry):
        @pl.when(r == rows - 1)
        def _():
            prepare(r, 0)

        x_sc[r] = attend_row(
            r,
            x_sc[r],
            bias,
            wo_sc[...],
            out_bias_sc[...],
            q_sc,
            k_sc,
            v_sc,
            gate_sc,
            gated_sc,
            heads,
            dim,
        )
        out_copy(r).start()
        return carry

    lax.fori_loop(0, rows, row_step, 0)

    logit_copy.wait_send()
    gain_copy.wait_send()
    shard_copy(0, low, (d, s_next)).wait_send()
    shard_copy(1, low, (other, s_next)).wait_send()

    def drain_x(t, carry):
        x_right_copy(t, own).wait_send()
        x_left_copy(t, own).wait_send()
        return carry

    def drain_rows(r, carry):
        @pl.when(r > 0)
        def _():
            msa_copy(r).wait_send()

        out_copy(r).wait()
        return carry

    for t in range(1, n_right + 1):
        z_right_copy(t, own).wait_send()
        far_right_copy(t, own).wait_send()
    for t in range(1, n_left + 1):
        z_left_copy(t, own).wait_send()
        far_left_copy(t, own).wait_send()
    lax.fori_loop(0, nz, drain_x, 0)
    far_copy(own).wait_send()
    lax.fori_loop(0, rows, drain_rows, 0)
    head_copy(0).wait_send()
    head_copy(1).wait_send()
    pair_copy(0).wait_send()
    for k in range(rows - 1):

        @pl.when(core == 1)
        def _(k=k):
            leg_copy(k).wait_send()
            pass_copy(k).wait_send()

        @pl.when(core == 0)
        def _(k=k):
            pair_copy(k + 1).wait_send()

    for r in range(rows):
        pair_copy(r).wait_recv()


NX, LOW = 4, 2


def body(
    ndap,
    ns,
    msa,
    pair,
    weights,
    w_out,
    logit,
    gain,
    pair_gain,
    offset,
    out_bias,
):
    _, rows, n, width = msa.shape
    pair_width, heads = logit.shape[1:]
    dim = width // heads
    nz = ndap // (NX * LOW)
    n_right, n_left = nz // 2, nz - 1 - nz // 2
    hbm = pl.BlockSpec(memory_space=pltpu.HBM)
    dma = pltpu.SemaphoreType.DMA
    operands = (msa, pair, weights, w_out, logit[0].T, gain, pair_gain, offset, out_bias)
    return pl.pallas_call(
        functools.partial(kernel, NX, nz, ns, heads, dim),
        out_shape=(
            jax.ShapeDtypeStruct(msa.shape, F32),
            jax.ShapeDtypeStruct(pair.shape, F32),
        ),
        in_specs=[hbm] * 9,
        out_specs=(hbm, hbm),
        scratch_shapes=[
            pltpu.VMEM((rows, n, width), F32),
            pltpu.VMEM((rows, n, pair_width), F32),
            pltpu.VMEM((width, 4 * width), BF16),
            pltpu.VMEM((width, width), BF16),
            pltpu.VMEM((1, width), F32),
            pltpu.VMEM((1, width), F32),
            pltpu.VMEM((1, width), F32),
            pltpu.VMEM((heads, pair_width), BF16),
            pltpu.VMEM((1, pair_width), F32),
            pltpu.VMEM((rows, heads * n), F32),
            pltpu.VMEM((rows, heads * n), BF16),
            pltpu.VMEM((2, rows, heads * n), BF16),
            pltpu.VMEM((rows - 1, n, pair_width), F32),
            pltpu.VMEM((NX * nz, 2 * rows, heads * n), BF16),
            pltpu.VMEM((rows, n, width), BF16),
            pltpu.VMEM((rows, heads * n, HALF), BF16),
            pltpu.VMEM((rows, heads * n, 2 * HALF), BF16),
            pltpu.VMEM((rows, n, width), F32),
            pltpu.VMEM((n, width), BF16),
            dma((rows + 6,)),
            dma((2,)),
            dma((2,)),
            dma((2,)),
            dma((2,)),
            dma((n_right,)),
            dma((n_right,)),
            dma((n_left,)),
            dma((n_left,)),
            dma((nz,)),
            dma((nz,)),
            dma((nz,)),
            dma((nz,)),
            dma((1,)),
            dma((1,)),
            dma((n_right,)),
            dma((n_right,)),
            dma((n_left,)),
            dma((n_left,)),
            dma((rows + 1,)),
            dma((rows + 1,)),
            dma((rows,)),
            dma((rows,)),
            dma((rows - 1,)),
            dma((rows - 1,)),
            dma((rows - 1,)),
            pltpu.SemaphoreType.REGULAR((4,)),
        ],
        compiler_params=pltpu.CompilerParams(
            collective_id=0, has_side_effects=True, vmem_limit_bytes=44 << 20
        ),
    )(*(pltpu.with_memory_space_constraint(operand, pltpu.HBM) for operand in operands))


def solution(mesh):
    wide = P("section", "dap", None, None)
    deep = P("section", None, None)
    flat = P("section", None)
    return jax.shard_map(
        functools.partial(body, mesh.shape["dap"], mesh.shape["section"]),
        mesh=mesh,
        in_specs=(wide, wide, deep, deep, deep, flat, flat, flat, flat),
        out_specs=(wide, wide),
        check_vma=False,
    )
```

```python
import functools

import jax
import jax.numpy as jnp
from jax import lax
from jax.experimental import pallas as pl
from jax.experimental.pallas import tpu as pltpu
from jax.sharding import PartitionSpec as P

EPSILON = 1e-05
MESH = pl.DeviceIdType.MESH
BF16 = jnp.bfloat16
F32 = jnp.float32
HALF = 128


def whiten(values):
    center = values - jnp.mean(values, axis=-1, keepdims=True)
    spread = jnp.mean(center * center, axis=-1, keepdims=True)
    return center * lax.rsqrt(spread + EPSILON)


def prepare_row(r, x, weights, gain, offset, q_sc, k_sc, v_sc, gate_sc, heads, dim):
    n, width = x.shape
    per_half = HALF // dim
    normed = (whiten(x) * gain).astype(BF16)
    member = lax.broadcasted_iota(jnp.int32, (n, HALF), 1) // dim

    def project(block):
        return jnp.dot(
            normed, weights[:, block * width : (block + 1) * width], preferred_element_type=F32
        )

    q_sc[r] = (project(0) * (1.0 / dim**0.5)).astype(BF16)
    keys = project(1)
    values = project(2)
    for h in range(heads):
        lanes = slice(h // per_half * HALF, (h // per_half + 1) * HALF)
        mine = member == h % per_half
        k_sc[r, h * n : (h + 1) * n, :] = jnp.where(mine, keys[:, lanes], 0.0).astype(BF16)
        v_sc[r, h * n : (h + 1) * n, :HALF] = jnp.where(mine, values[:, lanes], 0.0).astype(BF16)
    gate_sc[r] = jax.nn.sigmoid(project(3) + offset)


def attend_row(r, x, bias, w_out, out_bias, q_sc, k_sc, v_sc, gate_sc, gated_sc, heads, dim):
    n, width = x.shape
    per_half = HALF // dim
    for half in range(width // HALF):
        lanes = slice(half * HALF, (half + 1) * HALF)
        queries = q_sc[r, :, lanes]
        total = None
        for pair in range(per_half // 2):
            h = half * per_half + pair * 2
            scores = lax.dot_general(
                queries,
                k_sc[r, h * n : (h + 2) * n, :],
                (((1,), (1,)), ((), ())),
                preferred_element_type=F32,
            )
            probs = []
            for u in range(2):
                own = bias[:, :, (h + u) * n : (h + u + 1) * n].astype(F32).reshape(n, n)
                shifted = scores[:, u * n : (u + 1) * n] + own
                top = jnp.max(shifted, axis=-1, keepdims=True)
                probs.append(jnp.exp(shifted - top).astype(BF16))
            part = jnp.dot(
                jnp.concatenate(probs, axis=-1),
                v_sc[r, h * n : (h + 2) * n, :],
                preferred_element_type=F32,
            )
            total = part if total is None else total + part
        gated_sc[:, lanes] = (total[:, :HALF] / total[:, HALF:] * gate_sc[r, :, lanes]).astype(BF16)
    return x + (jnp.dot(gated_sc[...], w_out, preferred_element_type=F32) + out_bias)


def kernel(
    nx,
    nz,
    ns,
    heads,
    dim,
    msa_hbm,
    pair_hbm,
    weights_hbm,
    w_out_hbm,
    logit_hbm,
    gain_hbm,
    pair_gain_hbm,
    offset_hbm,
    out_bias_hbm,
    out_hbm,
    pair_out_hbm,
    x_sc,
    pair_sc,
    w_sc,
    wo_sc,
    gain_sc,
    offset_sc,
    out_bias_sc,
    next_logit,
    next_gain,
    shard,
    shard_half,
    stage,
    relay,
    bias,
    q_sc,
    k_sc,
    v_sc,
    gate_sc,
    gated_sc,
    local_sem,
    w_send,
    w_recv,
    b_send,
    b_recv,
    zr_send,
    zr_recv,
    zl_send,
    zl_recv,
    xr_send,
    xr_recv,
    xl_send,
    xl_recv,
    far_send,
    far_recv,
    fr_send,
    fr_recv,
    fl_send,
    fl_recv,
    m_send,
    m_recv,
    p_send,
    p_recv,
    leg_send,
    leg_recv,
    pass_send,
    entered,
):
    rows, n = x_sc.shape[0], x_sc.shape[1]
    n_right = nz // 2
    n_left = nz - 1 - n_right
    d = lax.axis_index("dap")
    s = lax.axis_index("section")
    ndap = nx * nz * 2
    x = lax.div(d, 2 * nz)
    z = lax.rem(lax.div(d, 2), nz)
    low = lax.rem(d, 2)
    base = d - 2 * z
    z_right = base + 2 * lax.rem(z + 1, nz)
    z_left = base + 2 * lax.rem(z + nz - 1, nz)
    z_right2 = base + 2 * lax.rem(z + 2, nz)
    z_left2 = base + 2 * lax.rem(z + nz - 2, nz)
    x_right = lax.rem(d + 2 * nz, ndap)
    x_left = lax.rem(d + ndap - 2 * nz, ndap)
    x_far = lax.rem(d + 4 * nz, ndap)
    other = d + 1 - 2 * low
    s_next = lax.rem(s + 1, ns)
    s_prev = lax.rem(s + ns - 1, ns)
    core = lax.rem(s, 2)
    y = 2 * lax.div(s, 2) + low
    y_back = lax.rem(y + ns - 3, ns)
    y_ahead = lax.rem(y + 3, ns)

    def chip(at, on_core):
        return (d - low + lax.rem(at, 2), 2 * lax.div(at, 2) + on_core)

    relay_to = chip(y_back, 1)
    relay_from = chip(y_ahead, 1)
    last_stop = chip(y_back, 0)

    def slot(dx, dz):
        return lax.rem(x + dx + nx, nx) * nz + lax.rem(z + dz + nz, nz)

    pair_in = pltpu.make_async_copy(pair_hbm.at[0], pair_sc, local_sem.at[rows])
    fetched = [
        pltpu.make_async_copy(src, dst, local_sem.at[rows + 1 + i])
        for i, (src, dst) in enumerate(
            (
                (weights_hbm.at[0], w_sc),
                (w_out_hbm.at[0], wo_sc),
                (gain_hbm, gain_sc),
                (offset_hbm, offset_sc),
                (out_bias_hbm, out_bias_sc),
            )
        )
    ]
    pair_in.start()
    for copy in fetched:
        copy.start()

    barrier = pltpu.get_barrier_semaphore()
    peers = (
        (x_right, s),
        (x_left, s),
        (x_far, s),
        (d, s_next),
        (d, s_prev),
        (other, s_next),
        (other, s_prev),
        relay_from,
    )
    for peer in peers:
        pl.semaphore_signal(barrier, inc=1, device_id=peer, device_id_type=MESH)

    @pl.when(core == 1)
    def _():
        pl.semaphore_signal(barrier, inc=1, device_id=relay_to, device_id_type=MESH)
        pl.semaphore_signal(barrier, inc=1, device_id=last_stop, device_id_type=MESH)

    along = (
        (z_right, z == nz - 1, 2),
        (z_right2, z >= nz - 2, 3),
        (z_left, z >= 1, 0),
        (z_left2, z >= 2, 1),
    )
    expected = len(peers) + 2 * core
    for peer, smaller, _ in along:
        expected = expected + jnp.where(smaller, 1, 0)

        @pl.when(jnp.logical_not(smaller))
        def _(peer=peer):
            pl.semaphore_signal(barrier, inc=1, device_id=(peer, s), device_id_type=MESH)

    pl.semaphore_wait(barrier, expected)
    for peer, smaller, mark in along:

        @pl.when(smaller)
        def _(peer=peer, mark=mark):
            pl.semaphore_signal(
                entered.at[mark], inc=1, device_id=(peer, s), device_id_type=MESH
            )

    def await_entry(index):
        @pl.when(jnp.logical_not(along[index][1]))
        def _():
            pl.semaphore_wait(entered.at[index], 1)

    def remote(src, dst, send, recv, peer):
        return pltpu.make_async_remote_copy(
            src_ref=src,
            dst_ref=dst,
            send_sem=send,
            recv_sem=recv,
            device_id=peer,
            device_id_type=MESH,
        )

    logit_copy = remote(logit_hbm, next_logit, w_send.at[0], w_recv.at[0], (d, s_prev))
    gain_copy = remote(pair_gain_hbm, next_gain, w_send.at[1], w_recv.at[1], (d, s_prev))
    logit_copy.start()
    gain_copy.start()

    def msa_copy(r):
        return remote(msa_hbm.at[0, r], x_sc.at[r], m_send.at[r], m_recv.at[r], (d, s_next))

    def head_copy(half):
        part = pl.ds(half * (n // 2), n // 2)
        return remote(
            msa_hbm.at[0, 0, part],
            x_sc.at[0, part],
            m_send.at[half * rows],
            m_recv.at[half * rows],
            (d, s_next),
        )

    def pair_copy(r):
        return remote(
            pair_hbm.at[0, r], pair_out_hbm.at[0, r], p_send.at[r], p_recv.at[r], (d, s_next)
        )

    def leg_copy(k):
        return remote(
            pair_hbm.at[0, k + 1], relay.at[k], leg_send.at[k], leg_recv.at[k], relay_to
        )

    def pass_copy(k):
        return remote(
            relay.at[k], pair_out_hbm.at[0, k + 1], pass_send.at[k], p_recv.at[k + 1], last_stop
        )

    def relay_step(k):
        @pl.when(core == 1)
        def _():
            leg_copy(k).wait_recv()
            pass_copy(k).start()
            if k + 2 < rows - 1:
                leg_copy(k + 2).start()

    head_copy(0).start()
    member = lax.broadcasted_iota(jnp.int32, (n, HALF), 1) // dim

    def ones_step(r, carry):
        for h in range(heads):
            mine = member == h % (HALF // dim)
            v_sc[r, h * n : (h + 1) * n, HALF:] = jnp.where(mine, 1.0, 0.0).astype(BF16)
        return carry

    lax.fori_loop(0, rows, ones_step, 0)
    pair_in.wait()
    for r in range(rows):
        pair_sc[r] = whiten(pair_sc[r])
    logit_copy.wait_recv()
    gain_copy.wait_recv()

    @pl.when(core == 1)
    def _():
        leg_copy(0).start()
        leg_copy(1).start()

    logits = next_logit[...]
    for r in range(rows):
        normed = (pair_sc[r] * next_gain[...]).astype(BF16)
        shard_row = lax.dot_general(
            logits, normed, (((1,), (1,)), ((), ())), preferred_element_type=F32
        )
        for h in range(heads):
            shard[r : r + 1, h * n : (h + 1) * n] = shard_row[h : h + 1, :]

    shard_half[...] = shard[...].astype(BF16)

    def shard_copy(index, row, peer):
        return remote(shard_half, stage.at[row], b_send.at[index], b_recv.at[row], peer)

    shard_copy(0, low, (d, s_next)).start()
    shard_copy(1, low, (other, s_next)).start()
    head_copy(1).start()
    msa_copy(1).start()
    msa_copy(2).start()

    @pl.when(core == 0)
    def _():
        msa_copy(3).start()
        for r in range(rows):
            pair_copy(r).start()

    shard_copy(0, 0, (d, s_next)).wait_recv()
    shard_copy(1, 1, (other, s_next)).wait_recv()
    own = slot(0, 0)
    bias[own] = jnp.concatenate([stage[0].astype(F32), stage[1].astype(F32)], axis=0).astype(BF16)

    def block_copy(send, recv, t, block, peer):
        return remote(bias.at[block], bias.at[block], send.at[t], recv.at[t], (peer, s))

    def z_right_copy(t, block):
        return block_copy(zr_send, zr_recv, t - 1, block, z_right if t % 2 else z_right2)

    def z_left_copy(t, block):
        return block_copy(zl_send, zl_recv, t - 1, block, z_left if t % 2 else z_left2)

    def x_right_copy(t, block):
        return block_copy(xr_send, xr_recv, t, block, x_right)

    def x_left_copy(t, block):
        return block_copy(xl_send, xl_recv, t, block, x_left)

    def far_copy(block):
        return block_copy(far_send, far_recv, 0, block, x_far)

    def far_right_copy(t, block):
        return block_copy(fr_send, fr_recv, t - 1, block, z_right if t % 2 else z_right2)

    def far_left_copy(t, block):
        return block_copy(fl_send, fl_recv, t - 1, block, z_left if t % 2 else z_left2)

    def send_on(right, left, at, below, above):
        for t in (at + 2, at + 1):
            if t <= n_right and below is not None:
                right(t, below).start()
            if t <= n_left and above is not None:
                left(t, above).start()

    def beside(index, block):
        x_right_copy(index, block).start()
        x_left_copy(index, block).start()

    far_copy(own).start()
    beside(0, own)
    await_entry(0)
    await_entry(1)
    send_on(z_right_copy, z_left_copy, 0, own, None)
    await_entry(2)
    await_entry(3)
    send_on(z_right_copy, z_left_copy, 0, None, own)

    def far_round(at):
        for t in (at + 2, at + 1):
            if t <= n_right:
                far_right_copy(t, slot(2, -t)).wait_recv()
                if t % 2 == 0:
                    send_on(far_right_copy, far_left_copy, t, slot(2, -t), None)
            if t <= n_left:
                far_left_copy(t, slot(2, t)).wait_recv()
                if t % 2 == 0:
                    send_on(far_right_copy, far_left_copy, t, None, slot(2, t))

    def near_round(at):
        for t in (at + 2, at + 1):
            if t <= n_right:
                z_right_copy(t, slot(0, -t)).wait_recv()
                if t % 2 == 0:
                    send_on(z_right_copy, z_left_copy, t, slot(0, -t), None)
                beside(t, slot(0, -t))
            if t <= n_left:
                z_left_copy(t, slot(0, t)).wait_recv()
                if t % 2 == 0:
                    send_on(z_right_copy, z_left_copy, t, None, slot(0, t))
                beside(n_right + t, slot(0, t))

    for copy in fetched:
        copy.wait()

    def prepare(r, carry):
        @pl.when(r == 0)
        def _():
            head_copy(0).wait_recv()
            head_copy(1).wait_recv()

        @pl.when(r > 0)
        def _():
            msa_copy(r).wait_recv()

        prepare_row(
            r, x_sc[r], w_sc, gain_sc[...], offset_sc[...], q_sc, k_sc, v_sc, gate_sc, heads, dim
        )
        return carry

    last = (n_right - 1) // 2 * 2
    for at in range(0, last + 1, 2):
        near_round(at)
        if at == 0:
            far = slot(2, 0)
            far_copy(far).wait_recv()
            send_on(far_right_copy, far_left_copy, 0, far, far)

            @pl.when(core == 1)
            def _():
                msa_copy(3).start()

        else:
            far_round(at - 2)
            relay_step(at // 2 - 1)
            if at == 2:
                prepare(0, 0)
    far_round(last)
    @pl.when(core == 1)
    def _():
        pair_copy(0).start()

    lax.fori_loop(1, rows - 1, prepare, 0)

    def finish(t, carry):
        below, above = jnp.where(t > n_right, 0, t), jnp.where(t > n_right, t - n_right, 0)
        x_right_copy(t, slot(-1, above - below)).wait_recv()
        x_left_copy(t, slot(1, above - below)).wait_recv()
        return carry

    lax.fori_loop(0, nz, finish, 0)

    def out_copy(r):
        return pltpu.make_async_copy(x_sc.at[r], out_hbm.at[0, r], local_sem.at[r])

    def row_step(r, carry):
        @pl.when(r == rows - 1)
        def _():
            prepare(r, 0)

        @pl.when(r == 1)
        def _():
            relay_step(2)

        x_sc[r] = attend_row(
            r,
            x_sc[r],
            bias,
            wo_sc[...],
            out_bias_sc[...],
            q_sc,
            k_sc,
            v_sc,
            gate_sc,
            gated_sc,
            heads,
            dim,
        )
        out_copy(r).start()
        return carry

    lax.fori_loop(0, rows, row_step, 0)

    logit_copy.wait_send()
    gain_copy.wait_send()
    shard_copy(0, low, (d, s_next)).wait_send()
    shard_copy(1, low, (other, s_next)).wait_send()

    def drain_x(t, carry):
        x_right_copy(t, own).wait_send()
        x_left_copy(t, own).wait_send()
        return carry

    def drain_rows(r, carry):
        @pl.when(r > 0)
        def _():
            msa_copy(r).wait_send()

        out_copy(r).wait()
        return carry

    for t in range(1, n_right + 1):
        z_right_copy(t, own).wait_send()
        far_right_copy(t, own).wait_send()
    for t in range(1, n_left + 1):
        z_left_copy(t, own).wait_send()
        far_left_copy(t, own).wait_send()
    lax.fori_loop(0, nz, drain_x, 0)
    far_copy(own).wait_send()
    lax.fori_loop(0, rows, drain_rows, 0)
    head_copy(0).wait_send()
    head_copy(1).wait_send()
    pair_copy(0).wait_send()
    for k in range(rows - 1):

        @pl.when(core == 1)
        def _(k=k):
            leg_copy(k).wait_send()
            pass_copy(k).wait_send()

        @pl.when(core == 0)
        def _(k=k):
            pair_copy(k + 1).wait_send()

    for r in range(rows):
        pair_copy(r).wait_recv()


NX, LOW = 4, 2


def body(
    ndap,
    ns,
    msa,
    pair,
    weights,
    w_out,
    logit,
    gain,
    pair_gain,
    offset,
    out_bias,
):
    _, rows, n, width = msa.shape
    pair_width, heads = logit.shape[1:]
    dim = width // heads
    nz = ndap // (NX * LOW)
    n_right, n_left = nz // 2, nz - 1 - nz // 2
    hbm = pl.BlockSpec(memory_space=pltpu.HBM)
    dma = pltpu.SemaphoreType.DMA
    operands = (msa, pair, weights, w_out, logit[0].T, gain, pair_gain, offset, out_bias)
    return pl.pallas_call(
        functools.partial(kernel, NX, nz, ns, heads, dim),
        out_shape=(
            jax.ShapeDtypeStruct(msa.shape, F32),
            jax.ShapeDtypeStruct(pair.shape, F32),
        ),
        in_specs=[hbm] * 9,
        out_specs=(hbm, hbm),
        scratch_shapes=[
            pltpu.VMEM((rows, n, width), F32),
            pltpu.VMEM((rows, n, pair_width), F32),
            pltpu.VMEM((width, 4 * width), BF16),
            pltpu.VMEM((width, width), BF16),
            pltpu.VMEM((1, width), F32),
            pltpu.VMEM((1, width), F32),
            pltpu.VMEM((1, width), F32),
            pltpu.VMEM((heads, pair_width), BF16),
            pltpu.VMEM((1, pair_width), F32),
            pltpu.VMEM((rows, heads * n), F32),
            pltpu.VMEM((rows, heads * n), BF16),
            pltpu.VMEM((2, rows, heads * n), BF16),
            pltpu.VMEM((rows - 1, n, pair_width), F32),
            pltpu.VMEM((NX * nz, 2 * rows, heads * n), BF16),
            pltpu.VMEM((rows, n, width), BF16),
            pltpu.VMEM((rows, heads * n, HALF), BF16),
            pltpu.VMEM((rows, heads * n, 2 * HALF), BF16),
            pltpu.VMEM((rows, n, width), F32),
            pltpu.VMEM((n, width), BF16),
            dma((rows + 6,)),
            dma((2,)),
            dma((2,)),
            dma((2,)),
            dma((2,)),
            dma((n_right,)),
            dma((n_right,)),
            dma((n_left,)),
            dma((n_left,)),
            dma((nz,)),
            dma((nz,)),
            dma((nz,)),
            dma((nz,)),
            dma((1,)),
            dma((1,)),
            dma((n_right,)),
            dma((n_right,)),
            dma((n_left,)),
            dma((n_left,)),
            dma((rows + 1,)),
            dma((rows + 1,)),
            dma((rows,)),
            dma((rows,)),
            dma((rows - 1,)),
            dma((rows - 1,)),
            dma((rows - 1,)),
            pltpu.SemaphoreType.REGULAR((4,)),
        ],
        compiler_params=pltpu.CompilerParams(
            collective_id=0, has_side_effects=True, vmem_limit_bytes=44 << 20
        ),
    )(*(pltpu.with_memory_space_constraint(operand, pltpu.HBM) for operand in operands))


def solution(mesh):
    wide = P("section", "dap", None, None)
    deep = P("section", None, None)
    flat = P("section", None)
    return jax.shard_map(
        functools.partial(body, mesh.shape["dap"], mesh.shape["section"]),
        mesh=mesh,
        in_specs=(wide, wide, deep, deep, deep, flat, flat, flat, flat),
        out_specs=(wide, wide),
        check_vma=False,
    )
```
